256 devices in a mesh: gx: 8 (over x, core), gy: 4 (over y), gz: 8 (over z).
Axes of the slice: x: 4, y: 4, z: 8, core: 2. Of those that a mesh axis runs over, the one named last changes fastest.
Arguments:
- left_core: float32 [256, 4096, 256], P(None, ('gx', 'gy', 'gz')), may hold values from -4000 to 4000
- right_core: float32 [256, 4096, 256], P(None, ('gx', 'gy', 'gz')), may hold values from -0.00012207031 to 0.00012207031
Outputs:
- left_out: float32 [256, 4096, 128], P(None, ('gx', 'gy', 'gz'))
- right_out: float32 [128, 4096, 256], P(None, ('gx', 'gy', 'gz'))
- next_factor: float32 [256, 256], replicated
The draws below stay inside these ranges and needn't reach their ends.
All inputs are finite; a program needn't handle non-finite values.
Results may differ from the reference program's by a relative error of at most 0.000075.
Values sent between devices are 32-bit elements; how exact they have to be, the bound alone decides.
A program may use at most 192 MiB of HBM per device.

```python
import math
import jax
import jax.numpy as jnp
from jax import lax

RL = 256
R = 256
RK = 128
RR = 256
NPTS = 4096


def draw_left_core(key, part):
    k_noise, k_cols, k_pts = jax.random.split(key, 3)
    base_noise = jnp.clip(jax.random.normal(k_noise, (RL, NPTS, R), jnp.float32), -6.0, 6.0)
    blended = base_noise + 0.5 * jnp.roll(base_noise, 1, axis=2)
    column_scale = jnp.exp(jax.random.uniform(k_cols, (R,), jnp.float32, 0.0, math.log(10.0)))
    rising = jnp.exp(math.log(3.0) * jnp.arange(NPTS, dtype=jnp.float32) / NPTS)
    point_scale = jnp.exp(jax.random.uniform(k_pts, (NPTS,), jnp.float32, 0.0, math.log(10.0))) * rising
    return blended * column_scale[None, None, :] * point_scale[None, :, None]


def levels(key, dims, shards, low, largest):
    level = 1.0
    for axis_at, parts in shards:
        draws = jax.random.uniform(jax.random.fold_in(jax.random.fold_in(key, 6), axis_at), (parts,), jnp.float32, low / len(shards), largest / len(shards))
        level = level * jnp.repeat(jnp.exp(draws), dims[axis_at] // parts).reshape((-1,) + (1,) * (len(dims) - 1 - axis_at))
    return level


def normal_values(own_key, dims, width, limit, cuts=(), kind=jnp.bfloat16):
    drawn = jax.random.normal(own_key, dims, jnp.float32) * width
    if len(cuts) > 0:
        drawn = levels(own_key, dims, cuts, -0.22, 0.18) * drawn
    return jnp.clip(drawn, min=-limit, max=limit).astype(kind)


def setup_inputs(seed: int = 0) -> dict:
    splits = jax.random.split(jax.random.key(seed), 3)
    return {
        "left_core": draw_left_core(jax.random.fold_in(splits[2], 71), 0),
        "right_core": normal_values(splits[1], (R, NPTS, RR), (RL * NPTS * 2048) ** -0.5, 0.00012207031, ((1, 256),), jnp.float32),
    }


def gram_of(matrix_rows):
    return lax.dot_general(matrix_rows.astype(jnp.float32), matrix_rows.astype(jnp.float32), (((0,), (0,)), ((), ())), precision=lax.Precision.HIGHEST, preferred_element_type=jnp.float32)

def reference(left_core, right_core):
    unfold = left_core.reshape(RL * NPTS, R)
    lower_full = jnp.linalg.cholesky(gram_of(unfold))
    upper = lower_full.T
    ortho_cols = lax.linalg.triangular_solve(lower_full[:RK, :RK], unfold[:, :RK], left_side=False, lower=True, transpose_a=True)
    left_out = (ortho_cols * math.sqrt(RL * NPTS)).reshape(RL, NPTS, RK)
    absorbed = jnp.dot(upper[:RK, :].astype(jnp.float32), right_core.reshape(R, NPTS * RR).astype(jnp.float32), precision=lax.Precision.HIGHEST, preferred_element_type=jnp.float32)
    right_out = absorbed.reshape(RK, NPTS, RR)
    next_gram = gram_of(absorbed.reshape(RK * NPTS, RR)) / (RK * NPTS)
    next_factor = jnp.linalg.cholesky(next_gram).T
    return (left_out, right_out, next_factor)
```

```python
import functools

import jax
import jax.numpy as jnp
from jax import lax
from jax.experimental import pallas as pl
from jax.experimental.pallas import tpu as pltpu
from jax.sharding import PartitionSpec as P

RK = 128
F32 = jnp.float32
BF16 = jnp.bfloat16
MESH = pl.DeviceIdType.MESH


def split(x):
    hi = x.astype(BF16)
    return hi, (x - hi.astype(F32)).astype(BF16)


def mm(a, b):
    return lax.dot_general(a, b, (((1,), (0,)), ((), ())), preferred_element_type=F32)


def mm_tn(a, b):
    return lax.dot_general(a, b, (((0,), (0,)), ((), ())), preferred_element_type=F32)


def gram_kernel(steps, x_ref, out_ref, acc, acc_lo):
    step = pl.program_id(0)
    hi, lo = split(x_ref[...])
    main = mm_tn(jnp.concatenate([hi[:, :RK], lo[:, :RK]], axis=1), hi)
    cross = mm_tn(hi[:, :RK], lo)
    part = main[:RK] + (main[RK:] + cross)

    @pl.when(step == 0)
    def _():
        acc[...] = part

    @pl.when(step > 0)
    def _():
        acc[...] += part

    @pl.when(step == steps - 1)
    def _():
        for half in range(2):
            out_ref[half * 16 : half * 16 + 16] = acc[:, half * RK : half * RK + RK].reshape(16, 1, 8, 128)


def local_gram(unfold):
    rows, cols = unfold.shape
    steps = 4
    return pl.pallas_call(
        functools.partial(gram_kernel, steps),
        grid=(steps,),
        out_shape=jax.ShapeDtypeStruct((32, 1, 8, 128), F32),
        in_specs=[pl.BlockSpec((rows // steps, cols), lambda i: (i, 0))],
        out_specs=pl.BlockSpec((32, 1, 8, 128), lambda i: (0, 0, 0, 0)),
        scratch_shapes=[pltpu.VMEM((RK, cols), F32), pltpu.VMEM((8, 128), F32)],
        compiler_params=pltpu.CompilerParams(vmem_limit_bytes=48 << 20),
        name="local_gram",
    )(unfold)


def sum_kernel(nx, ny, nz, src_ref, out_ref, rx, rz, s1, r1, s2, r2, s3, r3):
    gx, gy, gz = lax.axis_index("gx"), lax.axis_index("gy"), lax.axis_index("gz")
    n = nx * ny
    me = gx * ny + gy

    def plane(step):
        k = lax.rem(me + step, n)
        return k, (lax.div(k, ny), lax.rem(k, ny), gz)

    def line(step):
        return (gx, gy, lax.rem(gz + step, nz))

    barrier = pltpu.get_barrier_semaphore()

    @pl.loop(1, n)
    def _(s):
        pl.semaphore_signal(barrier, inc=1, device_id=plane(s)[1], device_id_type=MESH)

    @pl.loop(1, nz)
    def _(s):
        pl.semaphore_signal(barrier, inc=1, device_id=line(s), device_id_type=MESH)

    pl.semaphore_wait(barrier, n - 1 + nz - 1)

    def scatter(s):
        k, dev = plane(s)
        return pltpu.make_async_remote_copy(
            src_ref.at[k], rx.at[s], s1.at[s], r1.at[s], device_id=dev, device_id_type=MESH
        )

    def across(s):
        return pltpu.make_async_remote_copy(
            rz.at[gz], rz.at[gz], s2.at[s], r2.at[s], device_id=line(s), device_id_type=MESH
        )

    def gather(s):
        return pltpu.make_async_remote_copy(
            out_ref.at[me], out_ref.at[me], s3.at[s], r3.at[s], device_id=plane(s)[1], device_id_type=MESH
        )

    @pl.loop(1, n)
    def _(s):
        scatter(s).start()

    def take(s, acc):
        scatter(s).wait_recv()
        return acc + rx[s]

    rz[gz] = lax.fori_loop(1, n, take, src_ref[me])

    @pl.loop(1, nz)
    def _(s):
        across(s).start()

    @pl.loop(1, nz)
    def _(s):
        across(s).wait_recv()

    total = rz[0]
    for z in range(1, nz):
        total = total + rz[z]
    out_ref[me] = total

    @pl.loop(1, n)
    def _(s):
        gather(s).start()

    @pl.loop(1, n)
    def _(s):
        scatter(s).wait_send()

    @pl.loop(1, nz)
    def _(s):
        across(s).wait_send()

    @pl.loop(1, n)
    def _(s):
        gather(s).wait_recv()

    @pl.loop(1, n)
    def _(s):
        gather(s).wait_send()


def device_sum(src, sizes, ident):
    nx, ny, nz = sizes
    n = nx * ny
    tiles = src.shape[1]
    dma = pltpu.SemaphoreType.DMA
    return pl.pallas_call(
        functools.partial(sum_kernel, nx, ny, nz),
        out_shape=jax.ShapeDtypeStruct(src.shape, F32),
        in_specs=[pl.BlockSpec(memory_space=pltpu.VMEM)],
        out_specs=pl.BlockSpec(memory_space=pltpu.VMEM),
        scratch_shapes=[
            pltpu.VMEM((n, tiles, 8, 128), F32),
            pltpu.VMEM((nz, tiles, 8, 128), F32),
            dma((n,)), dma((n,)), dma((nz,)), dma((nz,)), dma((n,)), dma((n,)),
        ],
        compiler_params=pltpu.CompilerParams(collective_id=ident, has_side_effects=True),
        name="device_sum",
    )(src)


def rsqrt(x):
    r = lax.rsqrt(x)
    return r * (1.5 - 0.5 * x * r * r)


def eliminate(work, tiles):
    shape = (8, 128)
    for b in range(16):
        r0 = 8 * b
        rows8 = pl.ds(r0, 8)
        panel = [work[rows8, 128 * t : 128 * t + 128] for t in range(tiles)]

        def lanes(x):
            return [jnp.broadcast_to(x[:, r0 + k : r0 + k + 1], shape) for k in range(8)]

        cols = lanes(panel[0])
        e = [[jnp.broadcast_to(cols[k][i : i + 1, :], shape) if k <= i else None for k in range(8)] for i in range(8)]
        rows = [[jnp.broadcast_to(p[i : i + 1, :], shape) for i in range(8)] for p in panel]
        scale, mult = [], []
        for i in range(8):
            rs = rsqrt(e[i][i])
            l = [None] * 8
            for k in range(i + 1, 8):
                l[k] = e[k][i] * rs
            for k in range(i + 1, 8):
                for j in range(k, 8):
                    e[j][k] = e[j][k] - l[j] * l[k]
            scale.append(rs)
            mult.append(l)

        def apply(v):
            v = list(v)
            for i in range(8):
                v[i] = v[i] * scale[i]
                for k in range(i + 1, 8):
                    v[k] = v[k] - mult[i][k] * v[i]
            return v

        rows = [apply(r) for r in rows]
        sub = lax.broadcasted_iota(jnp.int32, shape, 0)
        for t in range(tiles):
            out = rows[t][0]
            for i in range(1, 8):
                out = jnp.where(sub == i, rows[t][i], out)
            work[rows8, 128 * t : 128 * t + 128] = out
        for m in range(b + 1, 16):
            m8 = pl.ds(8 * m, 8)
            cm = apply(lanes(work[m8, 0:128]))
            for t in range(tiles):
                v = work[m8, 128 * t : 128 * t + 128]
                for k in range(8):
                    v = v - cm[k] * rows[t][k]
                work[m8, 128 * t : 128 * t + 128] = v


def upper_mask():
    return lax.broadcasted_iota(jnp.int32, (128, 128), 0) <= lax.broadcasted_iota(jnp.int32, (128, 128), 1)


def identity():
    return jnp.where(
        lax.broadcasted_iota(jnp.int32, (128, 128), 0) == lax.broadcasted_iota(jnp.int32, (128, 128), 1), 1.0, 0.0
    ).astype(F32)


def cores_kernel(points, root, norm, g_ref, left_hbm, right_hbm, lo_hbm, ro_hbm, g2_ref,
                 work, lbuf, rbuf, lout, rout, sem):
    gets = [pltpu.make_async_copy(right_hbm.at[:, 128 * h : 128 * h + 128], rbuf.at[h], sem.at[h]) for h in range(2)]
    get_left = pltpu.make_async_copy(left_hbm.at[:, 0:128], lbuf, sem.at[4])
    for get in gets:
        get.start()
    get_left.start()
    work[:, 0:128] = g_ref[0:16].reshape(128, 128)
    work[:, 128:256] = g_ref[16:32].reshape(128, 128)
    work[:, 256:384] = identity()
    eliminate(work, 3)
    upper = jnp.concatenate([jnp.where(upper_mask(), work[:, 0:128], 0.0), work[:, 128:256]], axis=1)
    up_hi, up_lo = split(upper)
    up_both = jnp.concatenate([up_hi, up_lo], axis=0)
    for get in gets:
        get.wait()
    g_main = jnp.zeros((256, 256), F32)
    g_cross = jnp.zeros((256, 256), F32)
    for pair in range(points // 2):
        both = []
        for p in (2 * pair, 2 * pair + 1):
            at = pl.ds(p, 256, stride=points)
            r_hi, r_lo = split(jnp.concatenate([rbuf[0, at, :], rbuf[1, at, :]], axis=1))
            main = mm(up_both, r_hi)
            o = main[:128] + (main[128:] + mm(up_hi, r_lo))
            for h in range(2):
                rout[h, pl.ds(p, 128, stride=points), :] = o[:, 128 * h : 128 * h + 128]
            both.append(o)
        o_hi, o_lo = split(jnp.concatenate(both, axis=0))
        g_main = g_main + mm_tn(o_hi, o_hi)
        g_cross = g_cross + mm_tn(o_hi, o_lo)
    puts = [pltpu.make_async_copy(rout.at[h], ro_hbm.at[:, 128 * h : 128 * h + 128], sem.at[2 + h]) for h in range(2)]
    for put in puts:
        put.start()
    gram = (g_main + (g_cross + g_cross.T)) * norm
    for half in range(2):
        g2_ref[:, half] = gram[:, 128 * half : 128 * half + 128].reshape(32, 8, 128)
    w_hi, w_lo = split(work[:, 256:384].T * root)
    weights = jnp.concatenate(
        [jnp.concatenate([w_hi, w_lo], axis=1), jnp.concatenate([w_hi, jnp.zeros_like(w_lo)], axis=1)], axis=0
    )
    get_left.wait()
    rows = lbuf.shape[0]
    chunks = 4
    size = rows // chunks
    for c in range(chunks):
        at = pl.ds(c * size, size)
        x_hi, x_lo = split(lbuf[at, :])
        y = mm(jnp.concatenate([x_hi, x_lo], axis=1), weights)
        lout[at, :] = y[:, :128] + y[:, 128:]
        puts.append(pltpu.make_async_copy(lout.at[at, :], lo_hbm.at[at, :], sem.at[5 + c]))
        puts[-1].start()
    for put in puts:
        put.wait()


def new_cores(gram, left, right, points, root, norm):
    rows = left.shape[0]
    out_rows = RK * points
    any_spec = pl.BlockSpec(memory_space=pl.ANY)
    vmem_spec = pl.BlockSpec(memory_space=pltpu.VMEM)
    return pl.pallas_call(
        functools.partial(cores_kernel, points, root, norm),
        out_shape=(
            jax.ShapeDtypeStruct((rows, RK), F32),
            jax.ShapeDtypeStruct((out_rows, 256), F32),
            jax.ShapeDtypeStruct((32, 2, 8, 128), F32),
        ),
        in_specs=[vmem_spec, any_spec, any_spec],
        out_specs=(any_spec, any_spec, vmem_spec),
        scratch_shapes=[
            pltpu.VMEM((128, 384), F32),
            pltpu.VMEM((rows, RK), F32),
            pltpu.VMEM((2, right.shape[0], 128), F32),
            pltpu.VMEM((rows, RK), F32),
            pltpu.VMEM((2, out_rows, 128), F32),
            pltpu.SemaphoreType.DMA((9,)),
        ],
        compiler_params=pltpu.CompilerParams(vmem_limit_bytes=48 << 20),
        name="new_cores",
    )(gram, left, right)


def factor_kernel(g_ref, out_ref, work):
    work[:, 0:128] = g_ref[0:16, 0].reshape(128, 128)
    work[:, 128:256] = g_ref[0:16, 1].reshape(128, 128)
    eliminate(work, 2)
    right = work[:, 128:256]
    out_ref[0:128, 0:128] = jnp.where(upper_mask(), work[:, 0:128], 0.0)
    out_ref[0:128, 128:256] = right
    update = lax.dot_general(
        right, right, (((0,), (0,)), ((), ())), precision=lax.Precision.HIGHEST, preferred_element_type=F32
    )
    work[:, 0:128] = g_ref[16:32, 1].reshape(128, 128) - update
    eliminate(work, 1)
    out_ref[128:256, 0:128] = jnp.zeros((128, 128), F32)
    out_ref[128:256, 128:256] = jnp.where(upper_mask(), work[:, 0:128], 0.0)


def upper_factor(gram):
    return pl.pallas_call(
        factor_kernel,
        out_shape=jax.ShapeDtypeStruct((256, 256), F32),
        in_specs=[pl.BlockSpec(memory_space=pltpu.VMEM)],
        out_specs=pl.BlockSpec(memory_space=pltpu.VMEM),
        scratch_shapes=[pltpu.VMEM((128, 256), F32)],
        name="upper_factor",
    )(gram)


def per_device(left_core, right_core, sizes):
    rank_left, points, rank_mid = left_core.shape
    rank_right = right_core.shape[2]
    total_points = points * sizes[0] * sizes[1] * sizes[2]
    left = left_core.reshape(rank_left * points, rank_mid)
    right = right_core.reshape(rank_mid * points, rank_right)
    gram = device_sum(local_gram(left), sizes, 0)
    gram = gram.reshape(32, 8, 128)
    root = float(rank_left * total_points) ** 0.5
    norm = 1.0 / (RK * total_points)
    left_out, right_out, gram2 = new_cores(gram, left, right, points, root, norm)
    factor = upper_factor(device_sum(gram2, sizes, 1))
    return (
        left_out.reshape(rank_left, points, RK),
        right_out.reshape(RK, points, rank_right),
        factor,
    )


def solution(mesh):
    sizes = tuple(mesh.shape[a] for a in ("gx", "gy", "gz"))
    spec = P(None, ("gx", "gy", "gz"), None)
    return jax.shard_map(
        functools.partial(per_device, sizes=sizes),
        mesh=mesh, in_specs=(spec, spec), out_specs=(spec, spec, P()), check_vma=False,
    )
```

```python
import functools

import jax
import jax.numpy as jnp
from jax import lax
from jax.experimental import pallas as pl
from jax.experimental.pallas import tpu as pltpu
from jax.sharding import PartitionSpec as P

RK = 128
F32 = jnp.float32
BF16 = jnp.bfloat16
MESH = pl.DeviceIdType.MESH


def split(x):
    hi = x.astype(BF16)
    return hi, (x - hi.astype(F32)).astype(BF16)


def mm(a, b):
    return lax.dot_general(a, b, (((1,), (0,)), ((), ())), preferred_element_type=F32)


def mm_tn(a, b):
    return lax.dot_general(a, b, (((0,), (0,)), ((), ())), preferred_element_type=F32)


def exchange(sizes, src, out, rx, rz, sems, meanwhile):
    nx, ny, nz = sizes
    gx, gy, gz = lax.axis_index("gx"), lax.axis_index("gy"), lax.axis_index("gz")
    n = nx * ny
    me = gx * ny + gy

    def scatter(s):
        k, dev = plane(sizes, s)
        return pltpu.make_async_remote_copy(
            src.at[k], rx.at[s], sems.at[0, s], sems.at[1, s], device_id=dev, device_id_type=MESH
        )

    def across(s):
        return pltpu.make_async_remote_copy(
            rz.at[gz], rz.at[gz], sems.at[2, s], sems.at[3, s], device_id=line(sizes, s), device_id_type=MESH
        )

    def gather(s):
        return pltpu.make_async_remote_copy(
            out.at[me], out.at[me], sems.at[4, s], sems.at[5, s], device_id=plane(sizes, s)[1], device_id_type=MESH
        )

    @pl.loop(1, n)
    def _(s):
        scatter(s).start()

    meanwhile()

    def take(s, acc):
        scatter(s).wait_recv()
        return acc + rx[s]

    rz[gz] = lax.fori_loop(1, n, take, src[me])

    @pl.loop(1, nz)
    def _(s):
        across(s).start()

    @pl.loop(1, nz)
    def _(s):
        across(s).wait_recv()

    total = rz[0]
    for z in range(1, nz):
        total = total + rz[z]
    out[me] = total

    @pl.loop(1, n)
    def _(s):
        gather(s).start()

    @pl.loop(1, n)
    def _(s):
        gather(s).wait_recv()

    def finish():
        @pl.loop(1, n)
        def _(s):
            scatter(s).wait_send()
            gather(s).wait_send()

        @pl.loop(1, nz)
        def _(s):
            across(s).wait_send()

    return finish


def plane(sizes, step):
    n = sizes[0] * sizes[1]
    k = lax.rem(lax.axis_index("gx") * sizes[1] + lax.axis_index("gy") + step, n)
    return k, (lax.div(k, sizes[1]), lax.rem(k, sizes[1]), lax.axis_index("gz"))


def line(sizes, step):
    return (lax.axis_index("gx"), lax.axis_index("gy"), lax.rem(lax.axis_index("gz") + step, sizes[2]))


def rsqrt(x):
    r = lax.rsqrt(x)
    return r * (1.5 - 0.5 * x * r * r)


def eliminate(work, tiles):
    shape = (8, 128)
    for b in range(16):
        r0 = 8 * b
        rows8 = pl.ds(r0, 8)
        panel = [work[rows8, 128 * t : 128 * t + 128] for t in range(tiles)]

        def lanes(x):
            return [jnp.broadcast_to(x[:, r0 + k : r0 + k + 1], shape) for k in range(8)]

        cols = lanes(panel[0])
        e = [[jnp.broadcast_to(cols[k][i : i + 1, :], shape) if k <= i else None for k in range(8)] for i in range(8)]
        rows = [[jnp.broadcast_to(p[i : i + 1, :], shape) for i in range(8)] for p in panel]
        scale, mult = [], []
        for i in range(8):
            rs = rsqrt(e[i][i])
            l = [None] * 8
            for k in range(i + 1, 8):
                l[k] = e[k][i] * rs
            for k in range(i + 1, 8):
                for j in range(k, 8):
                    e[j][k] = e[j][k] - l[j] * l[k]
            scale.append(rs)
            mult.append(l)

        def apply(v):
            v = list(v)
            for i in range(8):
                v[i] = v[i] * scale[i]
                for k in range(i + 1, 8):
                    v[k] = v[k] - mult[i][k] * v[i]
            return v

        rows = [apply(r) for r in rows]
        sub = lax.broadcasted_iota(jnp.int32, shape, 0)
        for t in range(tiles):
            out = rows[t][0]
            for i in range(1, 8):
                out = jnp.where(sub == i, rows[t][i], out)
            work[rows8, 128 * t : 128 * t + 128] = out
        for m in range(b + 1, 16):
            m8 = pl.ds(8 * m, 8)
            cm = apply(lanes(work[m8, 0:128]))
            for t in range(tiles):
                v = work[m8, 128 * t : 128 * t + 128]
                for k in range(8):
                    v = v - cm[k] * rows[t][k]
                work[m8, 128 * t : 128 * t + 128] = v


def upper_mask():
    return lax.broadcasted_iota(jnp.int32, (128, 128), 0) <= lax.broadcasted_iota(jnp.int32, (128, 128), 1)


def identity():
    return jnp.where(
        lax.broadcasted_iota(jnp.int32, (128, 128), 0) == lax.broadcasted_iota(jnp.int32, (128, 128), 1), 1.0, 0.0
    ).astype(F32)


def whole_kernel(sizes, points, root, norm, left_hbm, right_hbm, lo_hbm, ro_hbm, f_ref,
                 lbuf, rbuf, r_hi, r_lo, lout, rout, work, src1, sum1, rx1, rz1, src2, sum2, rx2, rz2,
                 sems1, sems2, sem):
    nx, ny, nz = sizes
    rows = lbuf.shape[0]
    chunks = 4
    size = rows // chunks
    spans = [pl.ds(c * size, size) for c in range(chunks)]
    get_left = [pltpu.make_async_copy(left_hbm.at[at, :], lbuf.at[at, :], sem.at[c]) for c, at in enumerate(spans)]
    get_right = [
        pltpu.make_async_copy(right_hbm.at[:, 128 * h : 128 * h + 128], rbuf.at[h], sem.at[4 + h]) for h in range(2)
    ]
    for get in get_left + get_right:
        get.start()

    barrier = pltpu.get_barrier_semaphore()

    @pl.loop(1, nx * ny)
    def _(s):
        pl.semaphore_signal(barrier, inc=1, device_id=plane(sizes, s)[1], device_id_type=MESH)

    @pl.loop(1, nz)
    def _(s):
        pl.semaphore_signal(barrier, inc=1, device_id=line(sizes, s), device_id_type=MESH)

    gram = jnp.zeros((RK, 256), F32)
    for get, at in zip(get_left, spans):
        get.wait()
        hi, lo = split(lbuf[at, :])
        main = mm_tn(jnp.concatenate([hi[:, :RK], lo[:, :RK]], axis=1), hi)
        gram = gram + (main[:RK] + (main[RK:] + mm_tn(hi[:, :RK], lo)))
    for half in range(2):
        src1[half * 16 : half * 16 + 16] = gram[:, half * RK : half * RK + RK].reshape(16, 1, 8, 128)

    pl.semaphore_wait(barrier, nx * ny - 1 + nz - 1)

    def prepare_right():
        for get in get_right:
            get.wait()
        for p in range(points):
            at = pl.ds(p, 256, stride=points)
            for h in range(2):
                hi, lo = split(rbuf[h, at, :])
                r_hi[p, :, 128 * h : 128 * h + 128] = hi
                r_lo[p, :, 128 * h : 128 * h + 128] = lo

    finish1 = exchange(sizes, src1, sum1, rx1, rz1, sems1, prepare_right)

    work[:, 0:128] = sum1[0:16].reshape(128, 128)
    work[:, 128:256] = sum1[16:32].reshape(128, 128)
    work[:, 256:384] = identity()
    eliminate(work, 3)
    upper = jnp.concatenate([jnp.where(upper_mask(), work[:, 0:128], 0.0), work[:, 128:256]], axis=1)
    up_hi, up_lo = split(upper)
    up_both = jnp.concatenate([up_hi, up_lo], axis=0)
    g_main = jnp.zeros((256, 256), F32)
    g_cross = jnp.zeros((256, 256), F32)
    for pair in range(points // 2):
        both = []
        for p in (2 * pair, 2 * pair + 1):
            main = mm(up_both, r_hi[p])
            o = main[:128] + (main[128:] + mm(up_hi, r_lo[p]))
            for h in range(2):
                rout[h, pl.ds(p, 128, stride=points), :] = o[:, 128 * h : 128 * h + 128]
            both.append(o)
        o_hi, o_lo = split(jnp.concatenate(both, axis=0))
        g_main = g_main + mm_tn(o_hi, o_hi)
        g_cross = g_cross + mm_tn(o_hi, o_lo)
    put_right = [
        pltpu.make_async_copy(rout.at[h], ro_hbm.at[:, 128 * h : 128 * h + 128], sem.at[6 + h]) for h in range(2)
    ]
    for put in put_right:
        put.start()
    gram = (g_main + (g_cross + g_cross.T)) * norm
    for half in range(2):
        src2[:, half] = gram[:, 128 * half : 128 * half + 128].reshape(32, 8, 128)

    put_left = [pltpu.make_async_copy(lout.at[at, :], lo_hbm.at[at, :], sem.at[8 + c]) for c, at in enumerate(spans)]

    def make_left():
        w_hi, w_lo = split(work[:, 256:384].T * root)
        weights = jnp.concatenate(
            [jnp.concatenate([w_hi, w_lo], axis=1), jnp.concatenate([w_hi, jnp.zeros_like(w_lo)], axis=1)], axis=0
        )
        for put, at in zip(put_left, spans):
            x_hi, x_lo = split(lbuf[at, 0:128])
            y = mm(jnp.concatenate([x_hi, x_lo], axis=1), weights)
            lout[at, :] = y[:, :128] + y[:, 128:]
            put.start()

    finish2 = exchange(sizes, src2, sum2, rx2, rz2, sems2, make_left)

    work[:, 0:128] = sum2[0:16, 0].reshape(128, 128)
    work[:, 128:256] = sum2[0:16, 1].reshape(128, 128)
    eliminate(work, 2)
    right = work[:, 128:256]
    f_ref[0:128, 0:128] = jnp.where(upper_mask(), work[:, 0:128], 0.0)
    f_ref[0:128, 128:256] = right
    update = lax.dot_general(
        right, right, (((0,), (0,)), ((), ())), precision=lax.Precision.HIGHEST, preferred_element_type=F32
    )
    work[:, 0:128] = sum2[16:32, 1].reshape(128, 128) - update
    eliminate(work, 1)
    f_ref[128:256, 0:128] = jnp.zeros((128, 128), F32)
    f_ref[128:256, 128:256] = jnp.where(upper_mask(), work[:, 0:128], 0.0)
    for put in put_right + put_left:
        put.wait()
    finish1()
    finish2()


def whole(left, right, sizes, points, root, norm):
    rows = left.shape[0]
    out_rows = RK * points
    n, nz = sizes[0] * sizes[1], sizes[2]
    any_spec = pl.BlockSpec(memory_space=pl.ANY)
    return pl.pallas_call(
        functools.partial(whole_kernel, sizes, points, root, norm),
        out_shape=(
            jax.ShapeDtypeStruct((rows, RK), F32),
            jax.ShapeDtypeStruct((out_rows, 256), F32),
            jax.ShapeDtypeStruct((256, 256), F32),
        ),
        in_specs=[any_spec, any_spec],
        out_specs=(any_spec, any_spec, pl.BlockSpec(memory_space=pltpu.VMEM)),
        scratch_shapes=[
            pltpu.VMEM((rows, 256), F32),
            pltpu.VMEM((2, right.shape[0], 128), F32),
            pltpu.VMEM((points, 256, 256), BF16),
            pltpu.VMEM((points, 256, 256), BF16),
            pltpu.VMEM((rows, RK), F32),
            pltpu.VMEM((2, out_rows, 128), F32),
            pltpu.VMEM((128, 384), F32),
            pltpu.VMEM((32, 1, 8, 128), F32),
            pltpu.VMEM((32, 1, 8, 128), F32),
            pltpu.VMEM((n, 1, 8, 128), F32),
            pltpu.VMEM((nz, 1, 8, 128), F32),
            pltpu.VMEM((32, 2, 8, 128), F32),
            pltpu.VMEM((32, 2, 8, 128), F32),
            pltpu.VMEM((n, 2, 8, 128), F32),
            pltpu.VMEM((nz, 2, 8, 128), F32),
            pltpu.SemaphoreType.DMA((6, n)),
            pltpu.SemaphoreType.DMA((6, n)),
            pltpu.SemaphoreType.DMA((12,)),
        ],
        compiler_params=pltpu.CompilerParams(
            collective_id=0, has_side_effects=True, vmem_limit_bytes=56 << 20
        ),
        name="whole",
    )(left, right)


def per_device(left_core, right_core, sizes):
    rank_left, points, rank_mid = left_core.shape
    rank_right = right_core.shape[2]
    total_points = points * sizes[0] * sizes[1] * sizes[2]
    left = left_core.reshape(rank_left * points, rank_mid)
    right = right_core.reshape(rank_mid * points, rank_right)
    root = float(rank_left * total_points) ** 0.5
    norm = 1.0 / (RK * total_points)
    left_out, right_out, factor = whole(left, right, sizes, points, root, norm)
    return (
        left_out.reshape(rank_left, points, RK),
        right_out.reshape(RK, points, rank_right),
        factor,
    )


def solution(mesh):
    sizes = tuple(mesh.shape[a] for a in ("gx", "gy", "gz"))
    spec = P(None, ("gx", "gy", "gz"), None)
    return jax.shard_map(
        functools.partial(per_device, sizes=sizes),
        mesh=mesh, in_specs=(spec, spec), out_specs=(spec, spec, P()), check_vma=False,
    )
```

```python
import functools

import jax
import jax.numpy as jnp
from jax import lax
from jax.experimental import pallas as pl
from jax.experimental.pallas import tpu as pltpu
from jax.sharding import PartitionSpec as P

RK = 128
F32 = jnp.float32
BF16 = jnp.bfloat16
MESH = pl.DeviceIdType.MESH


def split(x):
    hi = x.astype(BF16)
    return hi, (x - hi.astype(F32)).astype(BF16)


def mm(a, b):
    return lax.dot_general(a, b, (((1,), (0,)), ((), ())), preferred_element_type=F32)


def mm_tn(a, b):
    return lax.dot_general(a, b, (((0,), (0,)), ((), ())), preferred_element_type=F32)


def exchange(sizes, src, out, rx, rz, sems, meanwhile):
    nx, ny, nz = sizes
    gx, gy, gz = lax.axis_index("gx"), lax.axis_index("gy"), lax.axis_index("gz")
    n = nx * ny
    me = gx * ny + gy

    def scatter(s):
        k, dev = plane(sizes, s)
        return pltpu.make_async_remote_copy(
            src.at[k], rx.at[s], sems.at[0, s], sems.at[1, s], device_id=dev, device_id_type=MESH
        )

    def across(s):
        return pltpu.make_async_remote_copy(
            rz.at[gz], rz.at[gz], sems.at[2, s], sems.at[3, s], device_id=line(sizes, s), device_id_type=MESH
        )

    def gather(s):
        return pltpu.make_async_remote_copy(
            out.at[me], out.at[me], sems.at[4, s], sems.at[5, s], device_id=plane(sizes, s)[1], device_id_type=MESH
        )

    @pl.loop(1, n)
    def _(s):
        scatter(s).start()

    meanwhile()

    def take(s, acc):
        scatter(s).wait_recv()
        return acc + rx[s]

    rz[gz] = lax.fori_loop(1, n, take, src[me])

    @pl.loop(1, nz)
    def _(s):
        across(s).start()

    @pl.loop(1, nz)
    def _(s):
        across(s).wait_recv()

    total = rz[0]
    for z in range(1, nz):
        total = total + rz[z]
    out[me] = total

    @pl.loop(1, n)
    def _(s):
        gather(s).start()

    @pl.loop(1, n)
    def _(s):
        gather(s).wait_recv()

    def finish():
        @pl.loop(1, n)
        def _(s):
            scatter(s).wait_send()
            gather(s).wait_send()

        @pl.loop(1, nz)
        def _(s):
            across(s).wait_send()

    return finish


def plane(sizes, step):
    n = sizes[0] * sizes[1]
    k = lax.rem(lax.axis_index("gx") * sizes[1] + lax.axis_index("gy") + step, n)
    return k, (lax.div(k, sizes[1]), lax.rem(k, sizes[1]), lax.axis_index("gz"))


def line(sizes, step):
    return (lax.axis_index("gx"), lax.axis_index("gy"), lax.rem(lax.axis_index("gz") + step, sizes[2]))


def eliminate(work, tiles):
    shape = (8, 128)
    for b in range(16):
        r0 = 8 * b
        rows8 = pl.ds(r0, 8)
        panel = [work[rows8, 128 * t : 128 * t + 128] for t in range(tiles)]

        def lanes(x):
            return [jnp.broadcast_to(x[:, r0 + k : r0 + k + 1], shape) for k in range(8)]

        cols = lanes(panel[0])
        e = [[jnp.broadcast_to(cols[k][i : i + 1, :], shape) if k <= i else None for k in range(8)] for i in range(8)]
        rows = [[jnp.broadcast_to(p[i : i + 1, :], shape) for i in range(8)] for p in panel]
        scale, mult = [], []
        for i in range(8):
            rs = lax.rsqrt(e[i][i])
            l = [None] * 8
            for k in range(i + 1, 8):
                l[k] = e[k][i] * rs
            for k in range(i + 1, 8):
                for j in range(k, 8):
                    e[j][k] = e[j][k] - l[j] * l[k]
            scale.append(rs)
            mult.append(l)

        def apply(v):
            v = list(v)
            for i in range(8):
                v[i] = v[i] * scale[i]
                for k in range(i + 1, 8):
                    v[k] = v[k] - mult[i][k] * v[i]
            return v

        rows = [apply(r) for r in rows]
        sub = lax.broadcasted_iota(jnp.int32, shape, 0)
        for t in range(tiles):
            out = rows[t][0]
            for i in range(1, 8):
                out = jnp.where(sub == i, rows[t][i], out)
            work[rows8, 128 * t : 128 * t + 128] = out
        for m in range(b + 1, 16):
            m8 = pl.ds(8 * m, 8)
            cm = apply(lanes(work[m8, 0:128]))
            for t in range(tiles):
                v = work[m8, 128 * t : 128 * t + 128]
                for k in range(8):
                    v = v - cm[k] * rows[t][k]
                work[m8, 128 * t : 128 * t + 128] = v


def upper_mask():
    return lax.broadcasted_iota(jnp.int32, (128, 128), 0) <= lax.broadcasted_iota(jnp.int32, (128, 128), 1)


def identity():
    return jnp.where(
        lax.broadcasted_iota(jnp.int32, (128, 128), 0) == lax.broadcasted_iota(jnp.int32, (128, 128), 1), 1.0, 0.0
    ).astype(F32)


def whole_kernel(sizes, points, root, norm, left_hbm, right_hbm, lout, rout, g2_ref,
                 lbuf, rbuf, r_hi, r_lo, work, src1, sum1, rx1, rz1, src2, sum2, rx2, rz2,
                 sems1, sems2, sem):
    nx, ny, nz = sizes
    rows = lbuf.shape[0]
    chunks = 4
    size = rows // chunks
    spans = [pl.ds(c * size, size) for c in range(chunks)]
    get_left = [pltpu.make_async_copy(left_hbm.at[at, :], lbuf.at[at, :], sem.at[c]) for c, at in enumerate(spans)]
    get_right = [
        pltpu.make_async_copy(right_hbm.at[:, 128 * h : 128 * h + 128], rbuf.at[h], sem.at[4 + h]) for h in range(2)
    ]
    for get in get_left + get_right:
        get.start()

    barrier = pltpu.get_barrier_semaphore()

    @pl.loop(1, nx * ny)
    def _(s):
        pl.semaphore_signal(barrier, inc=1, device_id=plane(sizes, s)[1], device_id_type=MESH)

    @pl.loop(1, nz)
    def _(s):
        pl.semaphore_signal(barrier, inc=1, device_id=line(sizes, s), device_id_type=MESH)

    gram = jnp.zeros((RK, 256), F32)
    for get, at in zip(get_left, spans):
        get.wait()
        hi, lo = split(lbuf[at, :])
        main = mm_tn(jnp.concatenate([hi[:, :RK], lo[:, :RK]], axis=1), hi)
        gram = gram + (main[:RK] + (main[RK:] + mm_tn(hi[:, :RK], lo)))
    for half in range(2):
        src1[half * 16 : half * 16 + 16] = gram[:, half * RK : half * RK + RK].reshape(16, 1, 8, 128)

    pl.semaphore_wait(barrier, nx * ny - 1 + nz - 1)

    def prepare_right():
        for get in get_right:
            get.wait()
        for p in range(points):
            at = pl.ds(p, 256, stride=points)
            for h in range(2):
                hi, lo = split(rbuf[h, at, :])
                r_hi[p, :, 128 * h : 128 * h + 128] = hi
                r_lo[p, :, 128 * h : 128 * h + 128] = lo

    finish1 = exchange(sizes, src1, sum1, rx1, rz1, sems1, prepare_right)

    work[:, 0:128] = sum1[0:16].reshape(128, 128)
    work[:, 128:256] = sum1[16:32].reshape(128, 128)
    work[:, 256:384] = identity()
    eliminate(work, 3)
    upper = jnp.concatenate([jnp.where(upper_mask(), work[:, 0:128], 0.0), work[:, 128:256]], axis=1)
    up_hi, up_lo = split(upper)
    up_both = jnp.concatenate([up_hi, up_lo], axis=0)
    g_main = jnp.zeros((256, 256), F32)
    g_cross = jnp.zeros((256, 256), F32)
    for pair in range(points // 2):
        both = []
        for p in (2 * pair, 2 * pair + 1):
            main = mm(up_both, r_hi[p])
            o = main[:128] + (main[128:] + mm(up_hi, r_lo[p]))
            for h in range(2):
                rout[h, pl.ds(p, 128, stride=points), :] = o[:, 128 * h : 128 * h + 128]
            both.append(o)
        o_hi, o_lo = split(jnp.concatenate(both, axis=0))
        g_main = g_main + mm_tn(o_hi, o_hi)
        g_cross = g_cross + mm_tn(o_hi, o_lo)
    gram = (g_main + (g_cross + g_cross.T)) * norm
    for half in range(2):
        src2[:, half] = gram[:, 128 * half : 128 * half + 128].reshape(32, 8, 128)

    def make_left():
        w_hi, w_lo = split(work[:, 256:384].T * root)
        weights = jnp.concatenate(
            [jnp.concatenate([w_hi, w_lo], axis=1), jnp.concatenate([w_hi, jnp.zeros_like(w_lo)], axis=1)], axis=0
        )
        for at in spans:
            x_hi, x_lo = split(lbuf[at, 0:128])
            y = mm(jnp.concatenate([x_hi, x_lo], axis=1), weights)
            lout[at, :] = y[:, :128] + y[:, 128:]

    finish2 = exchange(sizes, src2, sum2, rx2, rz2, sems2, make_left)

    g2_ref[...] = sum2[...]
    finish1()
    finish2()


def whole(left, right, sizes, points, root, norm):
    rows = left.shape[0]
    out_rows = RK * points
    n, nz = sizes[0] * sizes[1], sizes[2]
    any_spec = pl.BlockSpec(memory_space=pl.ANY)
    return pl.pallas_call(
        functools.partial(whole_kernel, sizes, points, root, norm),
        out_shape=(
            pltpu.VMEM((rows, RK), F32),
            pltpu.VMEM((2, out_rows, 128), F32),
            pltpu.VMEM((32, 2, 8, 128), F32),
        ),
        in_specs=[any_spec, any_spec],
        out_specs=(pl.BlockSpec(memory_space=pltpu.VMEM),) * 3,
        scratch_shapes=[
            pltpu.VMEM((rows, 256), F32),
            pltpu.VMEM((2, right.shape[0], 128), F32),
            pltpu.VMEM((points, 256, 256), BF16),
            pltpu.VMEM((points, 256, 256), BF16),
            pltpu.VMEM((128, 384), F32),
            pltpu.VMEM((32, 1, 8, 128), F32),
            pltpu.VMEM((32, 1, 8, 128), F32),
            pltpu.VMEM((n, 1, 8, 128), F32),
            pltpu.VMEM((nz, 1, 8, 128), F32),
            pltpu.VMEM((32, 2, 8, 128), F32),
            pltpu.VMEM((32, 2, 8, 128), F32),
            pltpu.VMEM((n, 2, 8, 128), F32),
            pltpu.VMEM((nz, 2, 8, 128), F32),
            pltpu.SemaphoreType.DMA((6, n)),
            pltpu.SemaphoreType.DMA((6, n)),
            pltpu.SemaphoreType.DMA((6,)),
        ],
        compiler_params=pltpu.CompilerParams(
            collective_id=0, has_side_effects=True, vmem_limit_bytes=56 << 20
        ),
        name="whole",
    )(left, right)


def factor_kernel(g_ref, lo_in, ro_in, f_ref, lo_out, ro_out, work, sem):
    puts = [pltpu.make_async_copy(lo_in, lo_out, sem.at[2])]
    for h in range(2):
        puts.append(pltpu.make_async_copy(ro_in.at[h], ro_out.at[:, 128 * h : 128 * h + 128], sem.at[h]))
    for put in puts:
        put.start()
    work[:, 0:128] = g_ref[0:16, 0].reshape(128, 128)
    work[:, 128:256] = g_ref[0:16, 1].reshape(128, 128)
    eliminate(work, 2)
    right = work[:, 128:256]
    f_ref[0:128, 0:128] = jnp.where(upper_mask(), work[:, 0:128], 0.0)
    f_ref[0:128, 128:256] = right
    update = lax.dot_general(
        right, right, (((0,), (0,)), ((), ())), precision=lax.Precision.HIGHEST, preferred_element_type=F32
    )
    work[:, 0:128] = g_ref[16:32, 1].reshape(128, 128) - update
    eliminate(work, 1)
    f_ref[128:256, 0:128] = jnp.zeros((128, 128), F32)
    f_ref[128:256, 128:256] = jnp.where(upper_mask(), work[:, 0:128], 0.0)
    for put in puts:
        put.wait()


def factor_and_place(gram, left_out, right_out):
    hbm_spec = pl.BlockSpec(memory_space=pltpu.HBM)
    vmem_spec = pl.BlockSpec(memory_space=pltpu.VMEM)
    return pl.pallas_call(
        factor_kernel,
        out_shape=(
            jax.ShapeDtypeStruct((256, 256), F32),
            jax.ShapeDtypeStruct(left_out.shape, F32),
            jax.ShapeDtypeStruct((right_out.shape[1], 256), F32),
        ),
        in_specs=[vmem_spec] * 3,
        out_specs=(vmem_spec, hbm_spec, hbm_spec),
        scratch_shapes=[pltpu.VMEM((128, 256), F32), pltpu.SemaphoreType.DMA((3,))],
        compiler_params=pltpu.CompilerParams(vmem_limit_bytes=8 << 20),
        name="factor_and_place",
    )(gram, left_out, right_out)


def per_device(left_core, right_core, sizes):
    rank_left, points, rank_mid = left_core.shape
    rank_right = right_core.shape[2]
    total_points = points * sizes[0] * sizes[1] * sizes[2]
    left = left_core.reshape(rank_left * points, rank_mid)
    right = right_core.reshape(rank_mid * points, rank_right)
    root = float(rank_left * total_points) ** 0.5
    norm = 1.0 / (RK * total_points)
    left_out, right_out, gram = whole(left, right, sizes, points, root, norm)
    factor, left_out, right_out = factor_and_place(gram, left_out, right_out)
    return (
        left_out.reshape(rank_left, points, RK),
        right_out.reshape(RK, points, rank_right),
        factor,
    )


def solution(mesh):
    sizes = tuple(mesh.shape[a] for a in ("gx", "gy", "gz"))
    spec = P(None, ("gx", "gy", "gz"), None)
    return jax.shard_map(
        functools.partial(per_device, sizes=sizes),
        mesh=mesh, in_specs=(spec, spec), out_specs=(spec, spec, P()), check_vma=False,
    )
```

```python
import functools

import jax
import jax.numpy as jnp
from jax import lax
from jax.experimental import pallas as pl
from jax.experimental.pallas import tpu as pltpu
from jax.sharding import PartitionSpec as P

RK = 128
F32 = jnp.float32
BF16 = jnp.bfloat16
MESH = pl.DeviceIdType.MESH
AXES = ("gx", "gy", "gz")


def split(x):
    hi = x.astype(BF16)
    return hi, (x - hi.astype(F32)).astype(BF16)


def mm(a, b):
    return lax.dot_general(a, b, (((1,), (0,)), ((), ())), preferred_element_type=F32)


def mm_tn(a, b):
    return lax.dot_general(a, b, (((0,), (0,)), ((), ())), preferred_element_type=F32)


def near(d, n):
    return min(d, n - d)


def plane(sizes):
    nx, ny, _ = sizes
    chips = nx // 2
    offsets = [(dx, dc, dy) for dx in range(chips) for dc in range(2) for dy in range(ny)][1:]
    offsets.sort(key=lambda o: -near(o[0], chips) - near(o[2], ny))
    gx, gy, gz = (lax.axis_index(a) for a in AXES)
    x, core = lax.div(gx, 2), lax.rem(gx, 2)
    xs = {(dx, dc): lax.rem(x + dx, chips) * 2 + lax.rem(core + dc, 2) for dx in range(chips) for dc in range(2)}
    ys = [lax.rem(gy + dy, ny) for dy in range(ny)]
    return [(xs[dx, dc] * ny + ys[dy], (xs[dx, dc], ys[dy], gz)) for dx, dc, dy in offsets]


def line(sizes):
    nz = sizes[2]
    gx, gy, gz = (lax.axis_index(a) for a in AXES)
    return [(gx, gy, lax.rem(gz + d, nz)) for d in sorted(range(1, nz), key=lambda d: -near(d, nz))]


def exchange(sizes, src, out, rx, rz, sems, meanwhile):
    nx, ny, nz = sizes
    n = nx * ny
    gz = lax.axis_index("gz")
    me = lax.axis_index("gx") * ny + lax.axis_index("gy")
    in_plane, in_line = plane(sizes), line(sizes)

    def copy(a, b, phase, dev):
        return pltpu.make_async_remote_copy(
            a, b, sems.at[2 * phase], sems.at[2 * phase + 1], device_id=dev, device_id_type=MESH
        )

    for s, (k, dev) in enumerate(in_plane):
        copy(src.at[k], rx.at[s], 0, dev).start()
    meanwhile()
    scatter = copy(rx, rx, 0, in_plane[0][1])
    scatter.wait_recv()
    total = src[me]
    for s in range(n - 1):
        total = total + rx[s]
    rz[gz] = total
    for dev in in_line:
        copy(rz.at[gz], rz.at[gz], 1, dev).start()
    rest = rz.at[pl.ds(0, nz - 1)]
    across = copy(rest, rest, 1, in_line[0])
    across.wait_recv()
    total = rz[0]
    for z in range(1, nz):
        total = total + rz[z]
    out[me] = total
    for _, dev in in_plane:
        copy(out.at[me], out.at[me], 2, dev).start()
    rest = out.at[pl.ds(0, n - 1)]
    gather = copy(rest, rest, 2, in_plane[0][1])
    gather.wait_recv()

    def finish():
        for waited in (scatter, across, gather):
            waited.wait_send()

    return finish


def eliminate(work, tiles):
    shape = (8, 128)
    for b in range(16):
        r0 = 8 * b
        rows8 = pl.ds(r0, 8)
        panel = [work[rows8, 128 * t : 128 * t + 128] for t in range(tiles)]

        def lanes(x):
            return [jnp.broadcast_to(x[:, r0 + k : r0 + k + 1], shape) for k in range(8)]

        cols = lanes(panel[0])
        e = [[jnp.broadcast_to(cols[k][i : i + 1, :], shape) if k <= i else None for k in range(8)] for i in range(8)]
        rows = [[jnp.broadcast_to(p[i : i + 1, :], shape) for i in range(8)] for p in panel]
        scale, mult = [], []
        for i in range(8):
            rs = lax.rsqrt(e[i][i])
            l = [None] * 8
            for k in range(i + 1, 8):
                l[k] = e[k][i] * rs
            for k in range(i + 1, 8):
                for j in range(k, 8):
                    e[j][k] = e[j][k] - l[j] * l[k]
            scale.append(rs)
            mult.append(l)

        def apply(v):
            v = list(v)
            for i in range(8):
                v[i] = v[i] * scale[i]
                for k in range(i + 1, 8):
                    v[k] = v[k] - mult[i][k] * v[i]
            return v

        rows = [apply(r) for r in rows]
        sub = lax.broadcasted_iota(jnp.int32, shape, 0)
        for t in range(tiles):
            out = rows[t][0]
            for i in range(1, 8):
                out = jnp.where(sub == i, rows[t][i], out)
            work[rows8, 128 * t : 128 * t + 128] = out
        for m in range(b + 1, 16):
            m8 = pl.ds(8 * m, 8)
            cm = apply(lanes(work[m8, 0:128]))
            for t in range(tiles):
                v = work[m8, 128 * t : 128 * t + 128]
                for k in range(8):
                    v = v - cm[k] * rows[t][k]
                work[m8, 128 * t : 128 * t + 128] = v


def upper_mask():
    return lax.broadcasted_iota(jnp.int32, (128, 128), 0) <= lax.broadcasted_iota(jnp.int32, (128, 128), 1)


def identity():
    return jnp.where(
        lax.broadcasted_iota(jnp.int32, (128, 128), 0) == lax.broadcasted_iota(jnp.int32, (128, 128), 1), 1.0, 0.0
    ).astype(F32)


def whole_kernel(sizes, points, root, norm, left_hbm, right_hbm, lout, rout, g2_ref,
                 lbuf, rbuf, r_hi, r_lo, work, src1, sum1, rx1, rz1, src2, sum2, rx2, rz2,
                 sems1, sems2, sem):
    nx, ny, nz = sizes
    rows = lbuf.shape[0]
    chunks = 4
    size = rows // chunks
    spans = [pl.ds(c * size, size) for c in range(chunks)]
    get_left = [pltpu.make_async_copy(left_hbm.at[at, :], lbuf.at[at, :], sem.at[c]) for c, at in enumerate(spans)]
    get_right = [
        pltpu.make_async_copy(right_hbm.at[:, 128 * h : 128 * h + 128], rbuf.at[h], sem.at[4 + h]) for h in range(2)
    ]
    for get in get_left + get_right:
        get.start()

    barrier = pltpu.get_barrier_semaphore()

    for dev in [dev for _, dev in plane(sizes)] + line(sizes):
        pl.semaphore_signal(barrier, inc=1, device_id=dev, device_id_type=MESH)

    gram = jnp.zeros((RK, 256), F32)
    for get, at in zip(get_left, spans):
        get.wait()
        hi, lo = split(lbuf[at, :])
        main = mm_tn(jnp.concatenate([hi[:, :RK], lo[:, :RK]], axis=1), hi)
        gram = gram + (main[:RK] + (main[RK:] + mm_tn(hi[:, :RK], lo)))
    for half in range(2):
        src1[half * 16 : half * 16 + 16] = gram[:, half * RK : half * RK + RK].reshape(16, 1, 8, 128)

    pl.semaphore_wait(barrier, nx * ny - 1 + nz - 1)

    def prepare_right():
        for get in get_right:
            get.wait()
        for p in range(points):
            at = pl.ds(p, 256, stride=points)
            for h in range(2):
                hi, lo = split(rbuf[h, at, :])
                r_hi[p, :, 128 * h : 128 * h + 128] = hi
                r_lo[p, :, 128 * h : 128 * h + 128] = lo

    finish1 = exchange(sizes, src1, sum1, rx1, rz1, sems1, prepare_right)

    work[:, 0:128] = sum1[0:16].reshape(128, 128)
    work[:, 128:256] = sum1[16:32].reshape(128, 128)
    work[:, 256:384] = identity()
    eliminate(work, 3)
    upper = jnp.concatenate([jnp.where(upper_mask(), work[:, 0:128], 0.0), work[:, 128:256]], axis=1)
    up_hi, up_lo = split(upper)
    up_both = jnp.concatenate([up_hi, up_lo], axis=0)
    g_main = jnp.zeros((256, 256), F32)
    g_cross = jnp.zeros((256, 256), F32)
    for pair in range(points // 2):
        both = []
        for p in (2 * pair, 2 * pair + 1):
            main = mm(up_both, r_hi[p])
            o = main[:128] + (main[128:] + mm(up_hi, r_lo[p]))
            for h in range(2):
                rout[h, pl.ds(p, 128, stride=points), :] = o[:, 128 * h : 128 * h + 128]
            both.append(o)
        o_hi, o_lo = split(jnp.concatenate(both, axis=0))
        g_main = g_main + mm_tn(o_hi, o_hi)
        g_cross = g_cross + mm_tn(o_hi, o_lo)
    gram = (g_main + (g_cross + g_cross.T)) * norm
    for half in range(2):
        src2[:, half] = gram[:, 128 * half : 128 * half + 128].reshape(32, 8, 128)

    def make_left():
        w_hi, w_lo = split(work[:, 256:384].T * root)
        weights = jnp.concatenate(
            [jnp.concatenate([w_hi, w_lo], axis=1), jnp.concatenate([w_hi, jnp.zeros_like(w_lo)], axis=1)], axis=0
        )
        for at in spans:
            x_hi, x_lo = split(lbuf[at, 0:128])
            y = mm(jnp.concatenate([x_hi, x_lo], axis=1), weights)
            lout[at, :] = y[:, :128] + y[:, 128:]

    finish2 = exchange(sizes, src2, sum2, rx2, rz2, sems2, make_left)

    g2_ref[...] = sum2[...]
    finish1()
    finish2()


def whole(left, right, sizes, points, root, norm):
    rows = left.shape[0]
    out_rows = RK * points
    n, nz = sizes[0] * sizes[1], sizes[2]
    any_spec = pl.BlockSpec(memory_space=pl.ANY)
    return pl.pallas_call(
        functools.partial(whole_kernel, sizes, points, root, norm),
        out_shape=(
            pltpu.VMEM((rows, RK), F32),
            pltpu.VMEM((2, out_rows, 128), F32),
            pltpu.VMEM((32, 2, 8, 128), F32),
        ),
        in_specs=[any_spec, any_spec],
        out_specs=(pl.BlockSpec(memory_space=pltpu.VMEM),) * 3,
        scratch_shapes=[
            pltpu.VMEM((rows, 256), F32),
            pltpu.VMEM((2, right.shape[0], 128), F32),
            pltpu.VMEM((points, 256, 256), BF16),
            pltpu.VMEM((points, 256, 256), BF16),
            pltpu.VMEM((128, 384), F32),
            pltpu.VMEM((32, 1, 8, 128), F32),
            pltpu.VMEM((32, 1, 8, 128), F32),
            pltpu.VMEM((n - 1, 1, 8, 128), F32),
            pltpu.VMEM((nz, 1, 8, 128), F32),
            pltpu.VMEM((32, 2, 8, 128), F32),
            pltpu.VMEM((32, 2, 8, 128), F32),
            pltpu.VMEM((n - 1, 2, 8, 128), F32),
            pltpu.VMEM((nz, 2, 8, 128), F32),
            pltpu.SemaphoreType.DMA((6,)),
            pltpu.SemaphoreType.DMA((6,)),
            pltpu.SemaphoreType.DMA((6,)),
        ],
        compiler_params=pltpu.CompilerParams(
            collective_id=0, has_side_effects=True, vmem_limit_bytes=56 << 20
        ),
        name="whole",
    )(left, right)


def factor_kernel(g_ref, lo_in, ro_in, f_ref, lo_out, ro_out, work, sem):
    puts = [pltpu.make_async_copy(lo_in, lo_out, sem.at[2])]
    for h in range(2):
        puts.append(pltpu.make_async_copy(ro_in.at[h], ro_out.at[:, 128 * h : 128 * h + 128], sem.at[h]))
    for put in puts:
        put.start()
    work[:, 0:128] = g_ref[0:16, 0].reshape(128, 128)
    work[:, 128:256] = g_ref[0:16, 1].reshape(128, 128)
    eliminate(work, 2)
    right = work[:, 128:256]
    f_ref[0:128, 0:128] = jnp.where(upper_mask(), work[:, 0:128], 0.0)
    f_ref[0:128, 128:256] = right
    update = lax.dot_general(
        right, right, (((0,), (0,)), ((), ())), precision=lax.Precision.HIGHEST, preferred_element_type=F32
    )
    work[:, 0:128] = g_ref[16:32, 1].reshape(128, 128) - update
    eliminate(work, 1)
    f_ref[128:256, 0:128] = jnp.zeros((128, 128), F32)
    f_ref[128:256, 128:256] = jnp.where(upper_mask(), work[:, 0:128], 0.0)
    for put in puts:
        put.wait()


def factor_and_place(gram, left_out, right_out):
    hbm_spec = pl.BlockSpec(memory_space=pltpu.HBM)
    vmem_spec = pl.BlockSpec(memory_space=pltpu.VMEM)
    return pl.pallas_call(
        factor_kernel,
        out_shape=(
            jax.ShapeDtypeStruct((256, 256), F32),
            jax.ShapeDtypeStruct(left_out.shape, F32),
            jax.ShapeDtypeStruct((right_out.shape[1], 256), F32),
        ),
        in_specs=[vmem_spec] * 3,
        out_specs=(vmem_spec, hbm_spec, hbm_spec),
        scratch_shapes=[pltpu.VMEM((128, 256), F32), pltpu.SemaphoreType.DMA((3,))],
        compiler_params=pltpu.CompilerParams(vmem_limit_bytes=8 << 20),
        name="factor_and_place",
    )(gram, left_out, right_out)


def per_device(left_core, right_core, sizes):
    rank_left, points, rank_mid = left_core.shape
    rank_right = right_core.shape[2]
    total_points = points * sizes[0] * sizes[1] * sizes[2]
    left = left_core.reshape(rank_left * points, rank_mid)
    right = right_core.reshape(rank_mid * points, rank_right)
    root = float(rank_left * total_points) ** 0.5
    norm = 1.0 / (RK * total_points)
    left_out, right_out, gram = whole(left, right, sizes, points, root, norm)
    factor, left_out, right_out = factor_and_place(gram, left_out, right_out)
    return (
        left_out.reshape(rank_left, points, RK),
        right_out.reshape(RK, points, rank_right),
        factor,
    )


def solution(mesh):
    sizes = tuple(mesh.shape[a] for a in ("gx", "gy", "gz"))
    spec = P(None, ("gx", "gy", "gz"), None)
    return jax.shard_map(
        functools.partial(per_device, sizes=sizes),
        mesh=mesh, in_specs=(spec, spec), out_specs=(spec, spec, P()), check_vma=False,
    )
```

```python
import functools

import jax
import jax.numpy as jnp
from jax import lax
from jax.experimental import pallas as pl
from jax.experimental.pallas import tpu as pltpu
from jax.sharding import PartitionSpec as P

RK = 128
F32 = jnp.float32
BF16 = jnp.bfloat16
MESH = pl.DeviceIdType.MESH
AXES = ("gx", "gy", "gz")


def split(x):
    hi = x.astype(BF16)
    return hi, (x - hi.astype(F32)).astype(BF16)


def mm(a, b):
    return lax.dot_general(a, b, (((1,), (0,)), ((), ())), preferred_element_type=F32)


def mm_tn(a, b):
    return lax.dot_general(a, b, (((0,), (0,)), ((), ())), preferred_element_type=F32)


def near(d, n):
    return min(d, n - d)


def plane(sizes):
    nx, ny, _ = sizes
    chips = nx // 2
    offsets = [(dx, dc, dy) for dx in range(chips) for dc in range(2) for dy in range(ny)][1:]
    offsets.sort(key=lambda o: -near(o[0], chips) - near(o[2], ny))
    gx, gy, gz = (lax.axis_index(a) for a in AXES)
    x, core = lax.div(gx, 2), lax.rem(gx, 2)
    xs = {(dx, dc): lax.rem(x + dx, chips) * 2 + lax.rem(core + dc, 2) for dx in range(chips) for dc in range(2)}
    ys = [lax.rem(gy + dy, ny) for dy in range(ny)]
    return [(xs[dx, dc] * ny + ys[dy], (xs[dx, dc], ys[dy], gz)) for dx, dc, dy in offsets]


def line(sizes):
    nz = sizes[2]
    gx, gy, gz = (lax.axis_index(a) for a in AXES)
    return [(gx, gy, lax.rem(gz + d, nz)) for d in sorted(range(1, nz), key=lambda d: -near(d, nz))]


def exchange(sizes, src, out, rx, rz, sems, first=None, last=None):
    nx, ny, nz = sizes
    n = nx * ny
    gz = lax.axis_index("gz")
    me = lax.axis_index("gx") * ny + lax.axis_index("gy")
    in_plane, in_line = plane(sizes), line(sizes)

    def copy(a, b, phase, dev):
        return pltpu.make_async_remote_copy(
            a, b, sems.at[2 * phase], sems.at[2 * phase + 1], device_id=dev, device_id_type=MESH
        )

    for s, (k, dev) in enumerate(in_plane):
        copy(src.at[k], rx.at[s], 0, dev).start()
    if first is not None:
        first()
    scatter = copy(rx, rx, 0, in_plane[0][1])
    scatter.wait_recv()
    total = src[me]
    for s in range(n - 1):
        total = total + rx[s]
    rz[gz] = total
    for dev in in_line:
        copy(rz.at[gz], rz.at[gz], 1, dev).start()
    rest = rz.at[pl.ds(0, nz - 1)]
    across = copy(rest, rest, 1, in_line[0])
    across.wait_recv()
    total = rz[0]
    for z in range(1, nz):
        total = total + rz[z]
    out[me] = total
    for _, dev in in_plane:
        copy(out.at[me], out.at[me], 2, dev).start()
    rest = out.at[pl.ds(0, n - 1)]
    gather = copy(rest, rest, 2, in_plane[0][1])
    if last is not None:
        last()
    gather.wait_recv()

    def finish():
        for waited in (scatter, across, gather):
            waited.wait_send()

    return finish


def eliminate(work, tiles):
    shape = (8, 128)
    sub = lax.broadcasted_iota(jnp.int32, shape, 0)

    def lane(x, c):
        return jnp.take_along_axis(x, jnp.full(shape, c, jnp.int32), axis=1)

    def row(x, i):
        return jnp.take_along_axis(x, jnp.full(shape, i, jnp.int32), axis=0)

    for b in range(16):
        r0 = 8 * b
        rows8 = pl.ds(r0, 8)
        panel = [work[rows8, 128 * t : 128 * t + 128] for t in range(tiles)]

        def lanes(x):
            return [lane(x, r0 + k) for k in range(8)]

        cols = lanes(panel[0])
        e = [[row(cols[k], i) if k <= i else None for k in range(8)] for i in range(8)]
        scale, mult = [], []
        for i in range(8):
            rs = lax.rsqrt(e[i][i])
            l = [None] * 8
            for k in range(i + 1, 8):
                l[k] = e[k][i] * rs
            for k in range(i + 1, 8):
                for j in range(k, 8):
                    e[j][k] = e[j][k] - l[j] * l[k]
            scale.append(rs)
            mult.append(l)

        def forward(v):
            v = list(v)
            for i in range(8):
                v[i] = v[i] * scale[i]
                for k in range(i + 1, 8):
                    v[k] = v[k] - mult[i][k] * v[i]
            return v

        def backward(v):
            v = list(v)
            for i in range(7, -1, -1):
                v[i] = v[i] * scale[i]
                for k in range(i):
                    v[k] = v[k] - mult[k][i] * v[i]
            return v

        rows = [forward([row(p, i) for i in range(8)]) for p in panel]
        for t in range(tiles):
            out = rows[t][0]
            for i in range(1, 8):
                out = jnp.where(sub == i, rows[t][i], out)
            work[rows8, 128 * t : 128 * t + 128] = out
        solved = [backward(r) for r in rows] if tiles > 1 else None
        for m in range(b + 1, 16):
            m8 = pl.ds(8 * m, 8)
            left = lanes(work[m8, 0:128])
            right = rows
            if m == b + 1 or solved is None:
                left = forward(left)
            else:
                right = solved
            for t in range(tiles):
                v = work[m8, 128 * t : 128 * t + 128]
                for k in range(8):
                    v = v - left[k] * right[t][k]
                work[m8, 128 * t : 128 * t + 128] = v


def upper_mask():
    return lax.broadcasted_iota(jnp.int32, (128, 128), 0) <= lax.broadcasted_iota(jnp.int32, (128, 128), 1)


def identity():
    return jnp.where(
        lax.broadcasted_iota(jnp.int32, (128, 128), 0) == lax.broadcasted_iota(jnp.int32, (128, 128), 1), 1.0, 0.0
    ).astype(F32)


def whole_kernel(sizes, points, root, norm, left_hbm, right_hbm, lout, rout, g2_ref,
                 lbuf, rbuf, r_hi, r_lo, o_hi, o_lo, work, src1, sum1, rx1, rz1, src2, sum2, rx2, rz2,
                 sems1, sems2, sem):
    nx, ny, nz = sizes
    rows = lbuf.shape[0]
    bounds = [0, rows // 8, rows * 5 // 16, rows * 19 // 32, rows]
    spans = [pl.ds(lo, hi - lo) for lo, hi in zip(bounds, bounds[1:])]
    get_left = [pltpu.make_async_copy(left_hbm.at[at, :], lbuf.at[at, :], sem.at[c]) for c, at in enumerate(spans)]
    get_right = [
        pltpu.make_async_copy(right_hbm.at[:, 128 * h : 128 * h + 128], rbuf.at[h], sem.at[4 + h]) for h in range(2)
    ]
    for get in get_left:
        get.start()

    barrier = pltpu.get_barrier_semaphore()

    for dev in [dev for _, dev in plane(sizes)] + line(sizes):
        pl.semaphore_signal(barrier, inc=1, device_id=dev, device_id_type=MESH)

    gram = jnp.zeros((RK, 256), F32)
    for get, at in zip(get_left, spans):
        get.wait()
        hi, lo = split(lbuf[at, :])
        main = mm_tn(jnp.concatenate([hi[:, :RK], lo[:, :RK]], axis=1), hi)
        gram = gram + (main[:RK] + (main[RK:] + mm_tn(hi[:, :RK], lo)))
    for get in get_right:
        get.start()
    for half in range(2):
        src1[half * 16 : half * 16 + 16] = gram[:, half * RK : half * RK + RK].reshape(16, 1, 8, 128)

    pl.semaphore_wait(barrier, nx * ny - 1 + nz - 1)

    def prepare_right():
        for get in get_right:
            get.wait()
        for p in range(points):
            at = pl.ds(p, 256, stride=points)
            for h in range(2):
                hi, lo = split(rbuf[h, at, :])
                r_hi[p, :, 128 * h : 128 * h + 128] = hi
                r_lo[p, :, 128 * h : 128 * h + 128] = lo

    finish1 = exchange(sizes, src1, sum1, rx1, rz1, sems1, last=prepare_right)

    work[:, 0:128] = sum1[0:16].reshape(128, 128)
    work[:, 128:256] = sum1[16:32].reshape(128, 128)
    work[:, 256:384] = identity()
    eliminate(work, 3)
    upper = jnp.concatenate([jnp.where(upper_mask(), work[:, 0:128], 0.0), work[:, 128:256]], axis=1)
    up_hi, up_lo = split(upper)
    up_both = jnp.concatenate([up_hi, up_lo], axis=0)
    for p in range(points):
        main = mm(up_both, r_hi[p])
        o = main[:128] + (main[128:] + mm(up_hi, r_lo[p]))
        for h in range(2):
            rout[h, pl.ds(p, 128, stride=points), :] = o[:, 128 * h : 128 * h + 128]
        at = pl.ds(128 * p, 128)
        o_hi[at, :], o_lo[at, :] = split(o)
    cross = mm_tn(o_hi[...], o_lo[...])
    gram = (mm_tn(o_hi[...], o_hi[...]) + (cross + cross.T)) * norm
    for half in range(2):
        src2[:, half] = gram[:, 128 * half : 128 * half + 128].reshape(32, 8, 128)

    def make_left():
        w_hi, w_lo = split(work[:, 256:384].T * root)
        weights = jnp.concatenate(
            [jnp.concatenate([w_hi, w_lo], axis=1), jnp.concatenate([w_hi, jnp.zeros_like(w_lo)], axis=1)], axis=0
        )
        for at in spans:
            x_hi, x_lo = split(lbuf[at, 0:128])
            y = mm(jnp.concatenate([x_hi, x_lo], axis=1), weights)
            lout[at, :] = y[:, :128] + y[:, 128:]

    finish2 = exchange(sizes, src2, sum2, rx2, rz2, sems2, first=make_left)

    g2_ref[...] = sum2[...]
    finish1()
    finish2()


def whole(left, right, sizes, points, root, norm):
    rows = left.shape[0]
    out_rows = RK * points
    n, nz = sizes[0] * sizes[1], sizes[2]
    any_spec = pl.BlockSpec(memory_space=pl.ANY)
    return pl.pallas_call(
        functools.partial(whole_kernel, sizes, points, root, norm),
        out_shape=(
            pltpu.VMEM((rows, RK), F32),
            pltpu.VMEM((2, out_rows, 128), F32),
            pltpu.VMEM((32, 2, 8, 128), F32),
        ),
        in_specs=[any_spec, any_spec],
        out_specs=(pl.BlockSpec(memory_space=pltpu.VMEM),) * 3,
        scratch_shapes=[
            pltpu.VMEM((rows, 256), F32),
            pltpu.VMEM((2, right.shape[0], 128), F32),
            pltpu.VMEM((points, 256, 256), BF16),
            pltpu.VMEM((points, 256, 256), BF16),
            pltpu.VMEM((out_rows, 256), BF16),
            pltpu.VMEM((out_rows, 256), BF16),
            pltpu.VMEM((128, 384), F32),
            pltpu.VMEM((32, 1, 8, 128), F32),
            pltpu.VMEM((32, 1, 8, 128), F32),
            pltpu.VMEM((n - 1, 1, 8, 128), F32),
            pltpu.VMEM((nz, 1, 8, 128), F32),
            pltpu.VMEM((32, 2, 8, 128), F32),
            pltpu.VMEM((32, 2, 8, 128), F32),
            pltpu.VMEM((n - 1, 2, 8, 128), F32),
            pltpu.VMEM((nz, 2, 8, 128), F32),
            pltpu.SemaphoreType.DMA((6,)),
            pltpu.SemaphoreType.DMA((6,)),
            pltpu.SemaphoreType.DMA((6,)),
        ],
        compiler_params=pltpu.CompilerParams(
            collective_id=0, has_side_effects=True, vmem_limit_bytes=56 << 20
        ),
        name="whole",
    )(left, right)


def factor_kernel(g_ref, lo_in, ro_in, f_ref, lo_out, ro_out, work, sem):
    puts = [pltpu.make_async_copy(lo_in, lo_out, sem.at[2])]
    for h in range(2):
        puts.append(pltpu.make_async_copy(ro_in.at[h], ro_out.at[:, 128 * h : 128 * h + 128], sem.at[h]))
    for put in puts:
        put.start()
    work[:, 0:128] = g_ref[0:16, 0].reshape(128, 128)
    work[:, 128:256] = g_ref[0:16, 1].reshape(128, 128)
    eliminate(work, 2)
    right = work[:, 128:256]
    f_ref[0:128, 0:128] = jnp.where(upper_mask(), work[:, 0:128], 0.0)
    f_ref[0:128, 128:256] = right
    update = lax.dot_general(
        right, right, (((0,), (0,)), ((), ())), precision=lax.Precision.HIGHEST, preferred_element_type=F32
    )
    work[:, 0:128] = g_ref[16:32, 1].reshape(128, 128) - update
    eliminate(work, 1)
    f_ref[128:256, 0:128] = jnp.zeros((128, 128), F32)
    f_ref[128:256, 128:256] = jnp.where(upper_mask(), work[:, 0:128], 0.0)
    for put in puts:
        put.wait()


def factor_and_place(gram, left_out, right_out):
    hbm_spec = pl.BlockSpec(memory_space=pltpu.HBM)
    vmem_spec = pl.BlockSpec(memory_space=pltpu.VMEM)
    return pl.pallas_call(
        factor_kernel,
        out_shape=(
            jax.ShapeDtypeStruct((256, 256), F32),
            jax.ShapeDtypeStruct(left_out.shape, F32),
            jax.ShapeDtypeStruct((right_out.shape[1], 256), F32),
        ),
        in_specs=[vmem_spec] * 3,
        out_specs=(vmem_spec, hbm_spec, hbm_spec),
        scratch_shapes=[pltpu.VMEM((128, 256), F32), pltpu.SemaphoreType.DMA((3,))],
        compiler_params=pltpu.CompilerParams(vmem_limit_bytes=8 << 20),
        name="factor_and_place",
    )(gram, left_out, right_out)


def per_device(left_core, right_core, sizes):
    rank_left, points, rank_mid = left_core.shape
    rank_right = right_core.shape[2]
    total_points = points * sizes[0] * sizes[1] * sizes[2]
    left = left_core.reshape(rank_left * points, rank_mid)
    right = right_core.reshape(rank_mid * points, rank_right)
    root = float(rank_left * total_points) ** 0.5
    norm = 1.0 / (RK * total_points)
    left_out, right_out, gram = whole(left, right, sizes, points, root, norm)
    factor, left_out, right_out = factor_and_place(gram, left_out, right_out)
    return (
        left_out.reshape(rank_left, points, RK),
        right_out.reshape(RK, points, rank_right),
        factor,
    )


def solution(mesh):
    sizes = tuple(mesh.shape[a] for a in ("gx", "gy", "gz"))
    spec = P(None, ("gx", "gy", "gz"), None)
    return jax.shard_map(
        functools.partial(per_device, sizes=sizes),
        mesh=mesh, in_specs=(spec, spec), out_specs=(spec, spec, P()), check_vma=False,
    )
```

```python
import functools

import jax
import jax.numpy as jnp
from jax import lax
from jax.experimental import pallas as pl
from jax.experimental.pallas import tpu as pltpu
from jax.sharding import PartitionSpec as P

RK = 128
F32 = jnp.float32
BF16 = jnp.bfloat16
MESH = pl.DeviceIdType.MESH
AXES = ("gx", "gy", "gz")


def split(x):
    hi = x.astype(BF16)
    return hi, (x - hi.astype(F32)).astype(BF16)


def mm(a, b):
    return lax.dot_general(a, b, (((1,), (0,)), ((), ())), preferred_element_type=F32)


def mm_tn(a, b):
    return lax.dot_general(a, b, (((0,), (0,)), ((), ())), preferred_element_type=F32)


def near(d, n):
    return min(d, n - d)


def plane(sizes):
    nx, ny, _ = sizes
    chips = nx // 2
    offsets = [(dx, dy) for dx in range(chips) for dy in range(ny)][1:]
    offsets.sort(key=lambda o: -near(o[0], chips) - near(o[1], ny))
    gx, gy, gz = (lax.axis_index(a) for a in AXES)
    x, core = lax.div(gx, 2), lax.rem(gx, 2)
    xs = [lax.rem(x + dx, chips) for dx in range(chips)]
    ys = [lax.rem(gy + dy, ny) for dy in range(ny)]
    return [(xs[dx] * ny + ys[dy], (xs[dx] * 2 + core, ys[dy], gz)) for dx, dy in offsets]


def line(sizes):
    nz = sizes[2]
    gx, gy, gz = (lax.axis_index(a) for a in AXES)
    return [(gx, gy, lax.rem(gz + d, nz)) for d in sorted(range(1, nz), key=lambda d: -near(d, nz))]


def partner():
    gx, gy, gz = (lax.axis_index(a) for a in AXES)
    return (gx + 1 - 2 * lax.rem(gx, 2), gy, gz)


def exchange(sizes, src, out, rc, part, rx, rz, sems, hooks):
    nx, ny, nz = sizes
    n = nx // 2 * ny
    gx, gz = lax.axis_index("gx"), lax.axis_index("gz")
    core = lax.rem(gx, 2)
    me = lax.div(gx, 2) * ny + lax.axis_index("gy")
    other, in_plane, in_line = partner(), plane(sizes), line(sizes)
    waits = []

    def copy(a, b, phase, dev):
        return pltpu.make_async_remote_copy(
            a, b, sems.at[2 * phase], sems.at[2 * phase + 1], device_id=dev, device_id_type=MESH
        )

    def receive(ref, phase, dev):
        if phase in hooks:
            hooks[phase]()
        waits.append(copy(ref, ref, phase, dev))
        waits[-1].wait_recv()

    copy(src.at[1 - core], rc, 0, other).start()
    receive(rc, 0, other)
    part[...] = src[core] + rc[...]
    for s, (k, dev) in enumerate(in_plane):
        copy(part.at[k], rx.at[s], 1, dev).start()
    receive(rx, 1, in_plane[0][1])
    total = part[me]
    for s in range(n - 1):
        total = total + rx[s]
    rz[gz] = total
    for dev in in_line:
        copy(rz.at[gz], rz.at[gz], 2, dev).start()
    receive(rz.at[pl.ds(0, nz - 1)], 2, in_line[0])
    total = rz[0]
    for z in range(1, nz):
        total = total + rz[z]
    out[core, me] = total
    for _, dev in in_plane:
        copy(out.at[core, me], out.at[core, me], 3, dev).start()
    receive(out.at[0, pl.ds(0, n - 1)], 3, in_plane[0][1])
    copy(out.at[core], out.at[core], 4, other).start()
    receive(out.at[0], 4, other)

    def finish():
        for waited in waits:
            waited.wait_send()

    return finish


def eliminate(work, tiles):
    shape = (8, 128)
    sub = lax.broadcasted_iota(jnp.int32, shape, 0)

    def lane(x, c):
        return jnp.take_along_axis(x, jnp.full(shape, c, jnp.int32), axis=1)

    def row(x, i):
        return jnp.take_along_axis(x, jnp.full(shape, i, jnp.int32), axis=0)

    for b in range(16):
        r0 = 8 * b
        rows8 = pl.ds(r0, 8)
        panel = [work[rows8, 128 * t : 128 * t + 128] for t in range(tiles)]

        def lanes(x):
            return [lane(x, r0 + k) for k in range(8)]

        cols = lanes(panel[0])
        e = [[row(cols[k], i) if k <= i else None for k in range(8)] for i in range(8)]
        scale, mult = [], []
        for i in range(8):
            rs = lax.rsqrt(e[i][i])
            l = [None] * 8
            for k in range(i + 1, 8):
                l[k] = e[k][i] * rs
            for k in range(i + 1, 8):
                for j in range(k, 8):
                    e[j][k] = e[j][k] - l[j] * l[k]
            scale.append(rs)
            mult.append(l)

        def forward(v):
            v = list(v)
            for i in range(8):
                v[i] = v[i] * scale[i]
                for k in range(i + 1, 8):
                    v[k] = v[k] - mult[i][k] * v[i]
            return v

        def backward(v):
            v = list(v)
            for i in range(7, -1, -1):
                v[i] = v[i] * scale[i]
                for k in range(i):
                    v[k] = v[k] - mult[k][i] * v[i]
            return v

        rows = [forward([row(p, i) for i in range(8)]) for p in panel]
        for t in range(tiles):
            out = rows[t][0]
            for i in range(1, 8):
                out = jnp.where(sub == i, rows[t][i], out)
            work[rows8, 128 * t : 128 * t + 128] = out
        solved = [backward(r) for r in rows] if tiles > 1 else None
        for m in range(b + 1, 16):
            m8 = pl.ds(8 * m, 8)
            left = lanes(work[m8, 0:128])
            right = rows
            if m == b + 1 or solved is None:
                left = forward(left)
            else:
                right = solved
            for t in range(tiles):
                v = work[m8, 128 * t : 128 * t + 128]
                for k in range(8):
                    v = v - left[k] * right[t][k]
                work[m8, 128 * t : 128 * t + 128] = v


def upper_mask():
    return lax.broadcasted_iota(jnp.int32, (128, 128), 0) <= lax.broadcasted_iota(jnp.int32, (128, 128), 1)


def identity():
    return jnp.where(
        lax.broadcasted_iota(jnp.int32, (128, 128), 0) == lax.broadcasted_iota(jnp.int32, (128, 128), 1), 1.0, 0.0
    ).astype(F32)


def whole_kernel(sizes, points, root, norm, left_hbm, right_hbm, lout, rout, g2_ref,
                 lbuf, rbuf, r_hi, r_lo, o_hi, o_lo, o_all, work,
                 src1, sum1, rc1, part1, rx1, rz1, src2, sum2, rc2, part2, rx2, rz2,
                 sems1, sems2, sem):
    nx, ny, nz = sizes
    rows = lbuf.shape[0]
    bounds = [0, rows // 8, rows * 5 // 16, rows * 19 // 32, rows]
    spans = [pl.ds(lo, hi - lo) for lo, hi in zip(bounds, bounds[1:])]
    get_left = [pltpu.make_async_copy(left_hbm.at[at, :], lbuf.at[at, :], sem.at[c]) for c, at in enumerate(spans)]
    get_right = [
        pltpu.make_async_copy(right_hbm.at[:, 128 * h : 128 * h + 128], rbuf.at[h], sem.at[4 + h]) for h in range(2)
    ]
    for get in get_left:
        get.start()

    barrier = pltpu.get_barrier_semaphore()

    for dev in [partner()] + [dev for _, dev in plane(sizes)] + line(sizes):
        pl.semaphore_signal(barrier, inc=1, device_id=dev, device_id_type=MESH)

    gram = jnp.zeros((RK, 256), F32)
    for get, at in zip(get_left, spans):
        get.wait()
        hi, lo = split(lbuf[at, :])
        main = mm_tn(jnp.concatenate([hi[:, :RK], lo[:, :RK]], axis=1), hi)
        gram = gram + (main[:RK] + (main[RK:] + mm_tn(hi[:, :RK], lo)))
    for get in get_right:
        get.start()
    for half in range(2):
        src1[half] = gram[:, half * RK : half * RK + RK].reshape(16, 1, 8, 128)

    pl.semaphore_wait(barrier, nx // 2 * ny + nz - 1)

    def prepare_right():
        for get in get_right:
            get.wait()
        for p in range(points):
            at = pl.ds(p, 256, stride=points)
            for h in range(2):
                hi, lo = split(rbuf[h, at, :])
                r_hi[p, :, 128 * h : 128 * h + 128] = hi
                r_lo[p, :, 128 * h : 128 * h + 128] = lo

    finish1 = exchange(sizes, src1, sum1, rc1, part1, rx1, rz1, sems1, {3: prepare_right})

    work[:, 0:128] = sum1[0].reshape(128, 128)
    work[:, 128:256] = sum1[1].reshape(128, 128)
    eliminate(work, 2)
    upper = jnp.concatenate([jnp.where(upper_mask(), work[:, 0:128], 0.0), work[:, 128:256]], axis=1)
    up_hi, up_lo = split(upper)
    up_both = jnp.concatenate([up_hi, up_lo], axis=0)
    for p in range(points):
        main = mm(up_both, r_hi[p])
        o = main[:128] + (main[128:] + mm(up_hi, r_lo[p]))
        at = pl.ds(128 * p, 128)
        o_all[at, :] = o
        o_hi[at, :], o_lo[at, :] = split(o)
    cross = mm_tn(o_hi[...], o_lo[...])
    gram = (mm_tn(o_hi[...], o_hi[...]) + (cross + cross.T)) * norm
    for half in range(2):
        src2[:, :, half] = gram[:, 128 * half : 128 * half + 128].reshape(2, 16, 8, 128)

    def invert():
        work[:, 0:128] = sum1[0].reshape(128, 128)
        work[:, 128:256] = identity()
        eliminate(work, 2)

    def place_right():
        for p in range(points):
            for h in range(2):
                rout[h, pl.ds(p, 128, stride=points), :] = o_all[128 * p : 128 * p + 128, 128 * h : 128 * h + 128]

    def make_left():
        w_hi, w_lo = split(work[:, 128:256].T * root)
        weights = jnp.concatenate(
            [jnp.concatenate([w_hi, w_lo], axis=1), jnp.concatenate([w_hi, jnp.zeros_like(w_lo)], axis=1)], axis=0
        )
        for at in spans:
            x_hi, x_lo = split(lbuf[at, 0:128])
            y = mm(jnp.concatenate([x_hi, x_lo], axis=1), weights)
            lout[at, :] = y[:, :128] + y[:, 128:]

    hooks = {1: invert, 2: place_right, 3: make_left}
    finish2 = exchange(sizes, src2, sum2, rc2, part2, rx2, rz2, sems2, hooks)
    g2_ref[...] = sum2[...]
    finish1()
    finish2()


def whole(left, right, sizes, points, root, norm):
    rows = left.shape[0]
    out_rows = RK * points
    n, nz = sizes[0] // 2 * sizes[1], sizes[2]
    any_spec = pl.BlockSpec(memory_space=pl.ANY)
    return pl.pallas_call(
        functools.partial(whole_kernel, sizes, points, root, norm),
        out_shape=(
            pltpu.VMEM((rows, RK), F32),
            pltpu.VMEM((2, out_rows, 128), F32),
            pltpu.VMEM((2, 16, 2, 8, 128), F32),
        ),
        in_specs=[any_spec, any_spec],
        out_specs=(pl.BlockSpec(memory_space=pltpu.VMEM),) * 3,
        scratch_shapes=[
            pltpu.VMEM((rows, 256), F32),
            pltpu.VMEM((2, right.shape[0], 128), F32),
            pltpu.VMEM((points, 256, 256), BF16),
            pltpu.VMEM((points, 256, 256), BF16),
            pltpu.VMEM((out_rows, 256), BF16),
            pltpu.VMEM((out_rows, 256), BF16),
            pltpu.VMEM((out_rows, 256), F32),
            pltpu.VMEM((128, 256), F32),
            *[
                pltpu.VMEM((*lead, tiles, 8, 128), F32)
                for tiles in (1, 2)
                for lead in ((2, n), (2, n), (n,), (n,), (n - 1,), (nz,))
            ],
            pltpu.SemaphoreType.DMA((10,)),
            pltpu.SemaphoreType.DMA((10,)),
            pltpu.SemaphoreType.DMA((6,)),
        ],
        compiler_params=pltpu.CompilerParams(
            collective_id=0, has_side_effects=True, vmem_limit_bytes=56 << 20
        ),
        name="whole",
    )(left, right)


def factor_kernel(g_ref, lo_in, ro_in, f_ref, lo_out, ro_out, work, sem):
    puts = [pltpu.make_async_copy(lo_in, lo_out, sem.at[2])]
    for h in range(2):
        puts.append(pltpu.make_async_copy(ro_in.at[h], ro_out.at[:, 128 * h : 128 * h + 128], sem.at[h]))
    for put in puts:
        put.start()
    work[:, 0:128] = g_ref[0, :, 0].reshape(128, 128)
    work[:, 128:256] = g_ref[0, :, 1].reshape(128, 128)
    eliminate(work, 2)
    right = work[:, 128:256]
    f_ref[0:128, 0:128] = jnp.where(upper_mask(), work[:, 0:128], 0.0)
    f_ref[0:128, 128:256] = right
    update = lax.dot_general(
        right, right, (((0,), (0,)), ((), ())), precision=lax.Precision.HIGHEST, preferred_element_type=F32
    )
    work[:, 0:128] = g_ref[1, :, 1].reshape(128, 128) - update
    eliminate(work, 1)
    f_ref[128:256, 0:128] = jnp.zeros((128, 128), F32)
    f_ref[128:256, 128:256] = jnp.where(upper_mask(), work[:, 0:128], 0.0)
    for put in puts:
        put.wait()


def factor_and_place(gram, left_out, right_out):
    hbm_spec = pl.BlockSpec(memory_space=pltpu.HBM)
    vmem_spec = pl.BlockSpec(memory_space=pltpu.VMEM)
    return pl.pallas_call(
        factor_kernel,
        out_shape=(
            jax.ShapeDtypeStruct((256, 256), F32),
            jax.ShapeDtypeStruct(left_out.shape, F32),
            jax.ShapeDtypeStruct((right_out.shape[1], 256), F32),
        ),
        in_specs=[vmem_spec] * 3,
        out_specs=(vmem_spec, hbm_spec, hbm_spec),
        scratch_shapes=[pltpu.VMEM((128, 256), F32), pltpu.SemaphoreType.DMA((3,))],
        compiler_params=pltpu.CompilerParams(vmem_limit_bytes=8 << 20),
        name="factor_and_place",
    )(gram, left_out, right_out)


def per_device(left_core, right_core, sizes):
    rank_left, points, rank_mid = left_core.shape
    rank_right = right_core.shape[2]
    total_points = points * sizes[0] * sizes[1] * sizes[2]
    left = left_core.reshape(rank_left * points, rank_mid)
    right = right_core.reshape(rank_mid * points, rank_right)
    root = float(rank_left * total_points) ** 0.5
    norm = 1.0 / (RK * total_points)
    left_out, right_out, gram = whole(left, right, sizes, points, root, norm)
    factor, left_out, right_out = factor_and_place(gram, left_out, right_out)
    return (
        left_out.reshape(rank_left, points, RK),
        right_out.reshape(RK, points, rank_right),
        factor,
    )


def solution(mesh):
    sizes = tuple(mesh.shape[a] for a in ("gx", "gy", "gz"))
    spec = P(None, ("gx", "gy", "gz"), None)
    return jax.shard_map(
        functools.partial(per_device, sizes=sizes),
        mesh=mesh, in_specs=(spec, spec), out_specs=(spec, spec, P()), check_vma=False,
    )
```

```python
import functools

import jax
import jax.numpy as jnp
from jax import lax
from jax.experimental import pallas as pl
from jax.experimental.pallas import tpu as pltpu
from jax.sharding import PartitionSpec as P

RK = 128
F32 = jnp.float32
BF16 = jnp.bfloat16
MESH = pl.DeviceIdType.MESH
AXES = ("gx", "gy", "gz")


def split(x):
    hi = x.astype(BF16)
    return hi, (x - hi.astype(F32)).astype(BF16)


def mm(a, b):
    return lax.dot_general(a, b, (((1,), (0,)), ((), ())), preferred_element_type=F32)


def mm_tn(a, b):
    return lax.dot_general(a, b, (((0,), (0,)), ((), ())), preferred_element_type=F32)


def nothing():
    pass


def near(d, n):
    return min(d, n - d)


def plane(sizes):
    nx, ny, _ = sizes
    chips = nx // 2
    offsets = [(dx, dc, dy) for dx in range(chips) for dc in range(2) for dy in range(ny)][1:]
    offsets.sort(key=lambda o: -near(o[0], chips) - near(o[2], ny))
    gx, gy, gz = (lax.axis_index(a) for a in AXES)
    x, core = lax.div(gx, 2), lax.rem(gx, 2)
    xs = {(dx, dc): lax.rem(x + dx, chips) * 2 + lax.rem(core + dc, 2) for dx in range(chips) for dc in range(2)}
    ys = [lax.rem(gy + dy, ny) for dy in range(ny)]
    return [(xs[dx, dc] * ny + ys[dy], (xs[dx, dc], ys[dy], gz)) for dx, dc, dy in offsets]


def line(sizes):
    nz = sizes[2]
    gx, gy, gz = (lax.axis_index(a) for a in AXES)
    return [(gx, gy, lax.rem(gz + d, nz)) for d in sorted(range(1, nz), key=lambda d: -near(d, nz))]


def exchange(sizes, src, out, rx, rz, sems, hooks):
    nx, ny, nz = sizes
    n = nx * ny
    gz = lax.axis_index("gz")
    me = lax.axis_index("gx") * ny + lax.axis_index("gy")
    in_plane, in_line = plane(sizes), line(sizes)

    def copy(a, b, phase, dev):
        return pltpu.make_async_remote_copy(
            a, b, sems.at[2 * phase], sems.at[2 * phase + 1], device_id=dev, device_id_type=MESH
        )

    for s, (k, dev) in enumerate(in_plane):
        copy(src.at[k], rx.at[s], 0, dev).start()
    hooks[0]()
    scatter = copy(rx, rx, 0, in_plane[0][1])
    scatter.wait_recv()
    total = src[me]
    for s in range(n - 1):
        total = total + rx[s]
    rz[gz] = total
    for dev in in_line:
        copy(rz.at[gz], rz.at[gz], 1, dev).start()
    rest = rz.at[pl.ds(0, nz - 1)]
    across = copy(rest, rest, 1, in_line[0])
    hooks[1]()
    across.wait_recv()
    total = rz[0]
    for z in range(1, nz):
        total = total + rz[z]
    out[me] = total
    for _, dev in in_plane:
        copy(out.at[me], out.at[me], 2, dev).start()
    rest = out.at[pl.ds(0, n - 1)]
    gather = copy(rest, rest, 2, in_plane[0][1])
    hooks[2]()
    gather.wait_recv()

    def finish():
        for waited in (scatter, across, gather):
            waited.wait_send()

    return finish


def eliminate(work, tiles):
    shape = (8, 128)
    sub = lax.broadcasted_iota(jnp.int32, shape, 0)

    def lane(x, c):
        return jnp.take_along_axis(x, jnp.full(shape, c, jnp.int32), axis=1)

    def row(x, i):
        return jnp.take_along_axis(x, jnp.full(shape, i, jnp.int32), axis=0)

    for b in range(16):
        r0 = 8 * b
        rows8 = pl.ds(r0, 8)
        panel = [work[rows8, 128 * t : 128 * t + 128] for t in range(tiles)]

        def lanes(x):
            return [lane(x, r0 + k) for k in range(8)]

        cols = lanes(panel[0])
        e = [[row(cols[k], i) if k <= i else None for k in range(8)] for i in range(8)]
        scale, mult = [], []
        for i in range(8):
            rs = lax.rsqrt(e[i][i])
            l = [None] * 8
            for k in range(i + 1, 8):
                l[k] = e[k][i] * rs
            for k in range(i + 1, 8):
                for j in range(k, 8):
                    e[j][k] = e[j][k] - l[j] * l[k]
            scale.append(rs)
            mult.append(l)

        def forward(v):
            v = list(v)
            for i in range(8):
                v[i] = v[i] * scale[i]
                for k in range(i + 1, 8):
                    v[k] = v[k] - mult[i][k] * v[i]
            return v

        def backward(v):
            v = list(v)
            for i in range(7, -1, -1):
                v[i] = v[i] * scale[i]
                for k in range(i):
                    v[k] = v[k] - mult[k][i] * v[i]
            return v

        rows = [forward([row(p, i) for i in range(8)]) for p in panel]
        for t in range(tiles):
            out = rows[t][0]
            for i in range(1, 8):
                out = jnp.where(sub == i, rows[t][i], out)
            work[rows8, 128 * t : 128 * t + 128] = out
        solved = [backward(r) for r in rows] if tiles > 1 else None
        for m in range(b + 1, 16):
            m8 = pl.ds(8 * m, 8)
            left = lanes(work[m8, 0:128])
            right = rows
            if m == b + 1 or solved is None:
                left = forward(left)
            else:
                right = solved
            for t in range(tiles):
                v = work[m8, 128 * t : 128 * t + 128]
                for k in range(8):
                    v = v - left[k] * right[t][k]
                work[m8, 128 * t : 128 * t + 128] = v


def upper_mask():
    return lax.broadcasted_iota(jnp.int32, (128, 128), 0) <= lax.broadcasted_iota(jnp.int32, (128, 128), 1)


def identity():
    return jnp.where(
        lax.broadcasted_iota(jnp.int32, (128, 128), 0) == lax.broadcasted_iota(jnp.int32, (128, 128), 1), 1.0, 0.0
    ).astype(F32)


def whole_kernel(sizes, points, root, norm, left_hbm, right_hbm, lout, rout, g2_ref,
                 lbuf, rbuf, r_hi, r_lo, o_hi, o_lo, o_all, work, src1, sum1, rx1, rz1, src2, sum2, rx2, rz2,
                 sems1, sems2, sem):
    nx, ny, nz = sizes
    rows = lbuf.shape[0]
    bounds = [0, rows // 8, rows * 5 // 16, rows * 19 // 32, rows]
    spans = [pl.ds(lo, hi - lo) for lo, hi in zip(bounds, bounds[1:])]
    get_left = [pltpu.make_async_copy(left_hbm.at[at, :], lbuf.at[at, :], sem.at[c]) for c, at in enumerate(spans)]
    get_right = [
        pltpu.make_async_copy(right_hbm.at[:, 128 * h : 128 * h + 128], rbuf.at[h], sem.at[4 + h]) for h in range(2)
    ]
    for get in get_left:
        get.start()

    barrier = pltpu.get_barrier_semaphore()

    for dev in [dev for _, dev in plane(sizes)] + line(sizes):
        pl.semaphore_signal(barrier, inc=1, device_id=dev, device_id_type=MESH)

    gram = jnp.zeros((RK, 256), F32)
    for get, at in zip(get_left, spans):
        get.wait()
        hi, lo = split(lbuf[at, :])
        main = mm_tn(jnp.concatenate([hi[:, :RK], lo[:, :RK]], axis=1), hi)
        gram = gram + (main[:RK] + (main[RK:] + mm_tn(hi[:, :RK], lo)))
    for get in get_right:
        get.start()
    for half in range(2):
        src1[half * 16 : half * 16 + 16] = gram[:, half * RK : half * RK + RK].reshape(16, 8, 128)

    pl.semaphore_wait(barrier, nx * ny - 1 + nz - 1)

    def prepare_right():
        for get in get_right:
            get.wait()
        for p in range(points):
            at = pl.ds(p, 256, stride=points)
            for h in range(2):
                hi, lo = split(rbuf[h, at, :])
                r_hi[p, :, 128 * h : 128 * h + 128] = hi
                r_lo[p, :, 128 * h : 128 * h + 128] = lo

    finish1 = exchange(sizes, src1, sum1, rx1, rz1, sems1, (nothing, nothing, prepare_right))

    work[:, 0:128] = sum1[0:16].reshape(128, 128)
    work[:, 128:256] = sum1[16:32].reshape(128, 128)
    eliminate(work, 2)
    upper = jnp.concatenate([jnp.where(upper_mask(), work[:, 0:128], 0.0), work[:, 128:256]], axis=1)
    up_hi, up_lo = split(upper)
    up_both = jnp.concatenate([up_hi, up_lo], axis=0)
    for p in range(points):
        main = mm(up_both, r_hi[p])
        o = main[:128] + (main[128:] + mm(up_hi, r_lo[p]))
        at = pl.ds(128 * p, 128)
        o_all[at, :] = o
        o_hi[at, :], o_lo[at, :] = split(o)
    cross = mm_tn(o_hi[...], o_lo[...])
    gram = (mm_tn(o_hi[...], o_hi[...]) + (cross + cross.T)) * norm
    for half in range(2):
        src2[16 * half : 16 * half + 16, 0:8] = gram[0:128, 128 * half : 128 * half + 128].reshape(16, 8, 128)
    for k in range(32):
        src2[k, 8:12] = gram[128 + 4 * k : 132 + 4 * k, 128:256]

    def invert():
        work[:, 0:128] = sum1[0:16].reshape(128, 128)
        work[:, 128:256] = identity()
        eliminate(work, 2)

    def place_right():
        for p in range(points):
            for h in range(2):
                rout[h, pl.ds(p, 128, stride=points), :] = o_all[128 * p : 128 * p + 128, 128 * h : 128 * h + 128]

    def make_left():
        w_hi, w_lo = split(work[:, 128:256].T * root)
        weights = jnp.concatenate(
            [jnp.concatenate([w_hi, w_lo], axis=1), jnp.concatenate([w_hi, jnp.zeros_like(w_lo)], axis=1)], axis=0
        )
        for at in spans:
            x_hi, x_lo = split(lbuf[at, 0:128])
            y = mm(jnp.concatenate([x_hi, x_lo], axis=1), weights)
            lout[at, :] = y[:, :128] + y[:, 128:]

    finish2 = exchange(sizes, src2, sum2, rx2, rz2, sems2, (invert, place_right, make_left))
    g2_ref[...] = sum2[...]
    finish1()
    finish2()


def whole(left, right, sizes, points, root, norm):
    rows = left.shape[0]
    out_rows = RK * points
    n, nz = sizes[0] * sizes[1], sizes[2]
    any_spec = pl.BlockSpec(memory_space=pl.ANY)
    return pl.pallas_call(
        functools.partial(whole_kernel, sizes, points, root, norm),
        out_shape=(
            pltpu.VMEM((rows, RK), F32),
            pltpu.VMEM((2, out_rows, 128), F32),
            pltpu.VMEM((n, 12, 128), F32),
        ),
        in_specs=[any_spec, any_spec],
        out_specs=(pl.BlockSpec(memory_space=pltpu.VMEM),) * 3,
        scratch_shapes=[
            pltpu.VMEM((rows, 256), F32),
            pltpu.VMEM((2, right.shape[0], 128), F32),
            pltpu.VMEM((points, 256, 256), BF16),
            pltpu.VMEM((points, 256, 256), BF16),
            pltpu.VMEM((out_rows, 256), BF16),
            pltpu.VMEM((out_rows, 256), BF16),
            pltpu.VMEM((out_rows, 256), F32),
            pltpu.VMEM((128, 256), F32),
            *[pltpu.VMEM((lead, high, 128), F32) for high in (8, 12) for lead in (n, n, n - 1, nz)],
            pltpu.SemaphoreType.DMA((6,)),
            pltpu.SemaphoreType.DMA((6,)),
            pltpu.SemaphoreType.DMA((6,)),
        ],
        compiler_params=pltpu.CompilerParams(
            collective_id=0, has_side_effects=True, vmem_limit_bytes=56 << 20
        ),
        name="whole",
    )(left, right)


def factor_kernel(g_ref, lo_in, ro_in, f_ref, lo_out, ro_out, work, corner, sem):
    puts = [pltpu.make_async_copy(lo_in, lo_out, sem.at[2])]
    for h in range(2):
        puts.append(pltpu.make_async_copy(ro_in.at[h], ro_out.at[:, 128 * h : 128 * h + 128], sem.at[h]))
    for put in puts:
        put.start()
    work[:, 0:128] = g_ref[0:16, 0:8].reshape(128, 128)
    work[:, 128:256] = g_ref[16:32, 0:8].reshape(128, 128)
    for k in range(32):
        corner[4 * k : 4 * k + 4, :] = g_ref[k, 8:12]
    eliminate(work, 2)
    right = work[:, 128:256]
    f_ref[0:128, 0:128] = jnp.where(upper_mask(), work[:, 0:128], 0.0)
    f_ref[0:128, 128:256] = right
    update = lax.dot_general(
        right, right, (((0,), (0,)), ((), ())), precision=lax.Precision.HIGHEST, preferred_element_type=F32
    )
    work[:, 0:128] = corner[...] - update
    eliminate(work, 1)
    f_ref[128:256, 0:128] = jnp.zeros((128, 128), F32)
    f_ref[128:256, 128:256] = jnp.where(upper_mask(), work[:, 0:128], 0.0)
    for put in puts:
        put.wait()


def factor_and_place(gram, left_out, right_out):
    hbm_spec = pl.BlockSpec(memory_space=pltpu.HBM)
    vmem_spec = pl.BlockSpec(memory_space=pltpu.VMEM)
    return pl.pallas_call(
        factor_kernel,
        out_shape=(
            jax.ShapeDtypeStruct((256, 256), F32),
            jax.ShapeDtypeStruct(left_out.shape, F32),
            jax.ShapeDtypeStruct((right_out.shape[1], 256), F32),
        ),
        in_specs=[vmem_spec] * 3,
        out_specs=(vmem_spec, hbm_spec, hbm_spec),
        scratch_shapes=[pltpu.VMEM((128, 256), F32), pltpu.VMEM((128, 128), F32), pltpu.SemaphoreType.DMA((3,))],
        compiler_params=pltpu.CompilerParams(vmem_limit_bytes=8 << 20),
        name="factor_and_place",
    )(gram, left_out, right_out)


def per_device(left_core, right_core, sizes):
    rank_left, points, rank_mid = left_core.shape
    rank_right = right_core.shape[2]
    total_points = points * sizes[0] * sizes[1] * sizes[2]
    left = left_core.reshape(rank_left * points, rank_mid)
    right = right_core.reshape(rank_mid * points, rank_right)
    root = float(rank_left * total_points) ** 0.5
    norm = 1.0 / (RK * total_points)
    left_out, right_out, gram = whole(left, right, sizes, points, root, norm)
    factor, left_out, right_out = factor_and_place(gram, left_out, right_out)
    return (
        left_out.reshape(rank_left, points, RK),
        right_out.reshape(RK, points, rank_right),
        factor,
    )


def solution(mesh):
    sizes = tuple(mesh.shape[a] for a in ("gx", "gy", "gz"))
    spec = P(None, ("gx", "gy", "gz"), None)
    return jax.shard_map(
        functools.partial(per_device, sizes=sizes),
        mesh=mesh, in_specs=(spec, spec), out_specs=(spec, spec, P()), check_vma=False,
    )
```

```python
import functools

import jax
import jax.numpy as jnp
from jax import lax
from jax.experimental import pallas as pl
from jax.experimental.pallas import tpu as pltpu
from jax.sharding import PartitionSpec as P

RK = 128
F32 = jnp.float32
BF16 = jnp.bfloat16
MESH = pl.DeviceIdType.MESH
AXES = ("gx", "gy", "gz")


def split(x):
    hi = x.astype(BF16)
    return hi, (x - hi.astype(F32)).astype(BF16)


def mm(a, b):
    return lax.dot_general(a, b, (((1,), (0,)), ((), ())), preferred_element_type=F32)


def mm_tn(a, b):
    return lax.dot_general(a, b, (((0,), (0,)), ((), ())), preferred_element_type=F32)


def nothing():
    pass


def near(d, n):
    return min(d, n - d)


def plane(sizes):
    nx, ny, _ = sizes
    chips = nx // 2
    offsets = [(dx, dc, dy) for dx in range(chips) for dc in range(2) for dy in range(ny)][1:]
    offsets.sort(key=lambda o: -near(o[0], chips) - near(o[2], ny))
    gx, gy, gz = (lax.axis_index(a) for a in AXES)
    x, core = lax.div(gx, 2), lax.rem(gx, 2)
    xs = {(dx, dc): lax.rem(x + dx, chips) * 2 + lax.rem(core + dc, 2) for dx in range(chips) for dc in range(2)}
    ys = [lax.rem(gy + dy, ny) for dy in range(ny)]
    return [(xs[dx, dc] * ny + ys[dy], (xs[dx, dc], ys[dy], gz)) for dx, dc, dy in offsets]


def line(sizes):
    nz = sizes[2]
    gx, gy, gz = (lax.axis_index(a) for a in AXES)
    return [(gx, gy, lax.rem(gz + d, nz)) for d in sorted(range(1, nz), key=lambda d: -near(d, nz))]


def exchange(sizes, src, out, rx, rz, sems, hooks):
    nx, ny, nz = sizes
    n = nx * ny
    gz = lax.axis_index("gz")
    me = lax.axis_index("gx") * ny + lax.axis_index("gy")
    in_plane, in_line = plane(sizes), line(sizes)

    def copy(a, b, phase, dev):
        return pltpu.make_async_remote_copy(
            a, b, sems.at[2 * phase], sems.at[2 * phase + 1], device_id=dev, device_id_type=MESH
        )

    for s, (k, dev) in enumerate(in_plane):
        copy(src.at[k], rx.at[s], 0, dev).start()
    hooks[0]()
    scatter = copy(rx, rx, 0, in_plane[0][1])
    scatter.wait_recv()
    total = src[me]
    for s in range(n - 1):
        total = total + rx[s]
    rz[gz] = total
    for dev in in_line:
        copy(rz.at[gz], rz.at[gz], 1, dev).start()
    rest = rz.at[pl.ds(0, nz - 1)]
    across = copy(rest, rest, 1, in_line[0])
    hooks[1]()
    across.wait_recv()
    total = rz[0]
    for z in range(1, nz):
        total = total + rz[z]
    out[me] = total
    for _, dev in in_plane:
        copy(out.at[me], out.at[me], 2, dev).start()
    rest = out.at[pl.ds(0, n - 1)]
    gather = copy(rest, rest, 2, in_plane[0][1])
    hooks[2]()
    gather.wait_recv()

    def finish():
        for waited in (scatter, across, gather):
            waited.wait_send()

    return finish


def eliminate(work, tiles):
    shape = (8, 128)
    sub = lax.broadcasted_iota(jnp.int32, shape, 0)

    def lane(x, c):
        return jnp.take_along_axis(x, jnp.full(shape, c, jnp.int32), axis=1)

    def row(x, i):
        return jnp.take_along_axis(x, jnp.full(shape, i, jnp.int32), axis=0)

    for b in range(16):
        r0 = 8 * b
        rows8 = pl.ds(r0, 8)
        panel = [work[rows8, 128 * t : 128 * t + 128] for t in range(tiles)]

        def lanes(x):
            return [lane(x, r0 + k) for k in range(8)]

        cols = lanes(panel[0])
        e = [[row(cols[k], i) if k <= i else None for k in range(8)] for i in range(8)]
        scale, mult = [], []
        for i in range(8):
            rs = lax.rsqrt(e[i][i])
            l = [None] * 8
            for k in range(i + 1, 8):
                l[k] = e[k][i] * rs
            for k in range(i + 1, 8):
                for j in range(k, 8):
                    e[j][k] = e[j][k] - l[j] * l[k]
            scale.append(rs)
            mult.append(l)

        def forward(v):
            v = list(v)
            for i in range(8):
                v[i] = v[i] * scale[i]
                for k in range(i + 1, 8):
                    v[k] = v[k] - mult[i][k] * v[i]
            return v

        def backward(v):
            v = list(v)
            for i in range(7, -1, -1):
                v[i] = v[i] * scale[i]
                for k in range(i):
                    v[k] = v[k] - mult[k][i] * v[i]
            return v

        rows = [forward([row(p, i) for i in range(8)]) for p in panel]
        for t in range(tiles):
            out = rows[t][0]
            for i in range(1, 8):
                out = jnp.where(sub == i, rows[t][i], out)
            work[rows8, 128 * t : 128 * t + 128] = out
        solved = [backward(r) for r in rows] if tiles > 1 else None
        for m in range(b + 1, 16):
            m8 = pl.ds(8 * m, 8)
            left = lanes(work[m8, 0:128])
            right = rows
            if m == b + 1 or solved is None:
                left = forward(left)
            else:
                right = solved
            for t in range(tiles):
                v = work[m8, 128 * t : 128 * t + 128]
                for k in range(8):
                    v = v - left[k] * right[t][k]
                work[m8, 128 * t : 128 * t + 128] = v


def upper_mask():
    return lax.broadcasted_iota(jnp.int32, (128, 128), 0) <= lax.broadcasted_iota(jnp.int32, (128, 128), 1)


def identity():
    return jnp.where(
        lax.broadcasted_iota(jnp.int32, (128, 128), 0) == lax.broadcasted_iota(jnp.int32, (128, 128), 1), 1.0, 0.0
    ).astype(F32)


def whole_kernel(sizes, points, root, norm, left_hbm, right_hbm, lout, rout, g2_ref,
                 lbuf, rbuf, r_hi, r_lo, o_hi, o_lo, o_all, work, src1, sum1, rx1, rz1, src2, rx2, rz2,
                 sems1, sems2, sem):
    nx, ny, nz = sizes
    rows = lbuf.shape[0]
    bounds = [0, rows // 8, rows * 5 // 16, rows * 19 // 32, rows]
    spans = [pl.ds(lo, hi - lo) for lo, hi in zip(bounds, bounds[1:])]
    get_left = [pltpu.make_async_copy(left_hbm.at[at, :], lbuf.at[at, :], sem.at[c]) for c, at in enumerate(spans)]
    get_right = [
        pltpu.make_async_copy(right_hbm.at[:, 128 * h : 128 * h + 128], rbuf.at[h], sem.at[4 + h]) for h in range(2)
    ]
    for get in get_left:
        get.start()

    barrier = pltpu.get_barrier_semaphore()

    for dev in [dev for _, dev in plane(sizes)] + line(sizes):
        pl.semaphore_signal(barrier, inc=1, device_id=dev, device_id_type=MESH)

    gram = jnp.zeros((RK, 256), F32)
    for get, at in zip(get_left, spans):
        get.wait()
        hi, lo = split(lbuf[at, :])
        both = jnp.concatenate([hi[:, :RK], lo[:, :RK]], axis=1)
        main, cross = mm_tn(both, hi), mm_tn(both, lo)
        gram = gram + (main[:RK] + (main[RK:] + cross[:RK] + cross[RK:]))
    for get in get_right:
        get.start()
    for half in range(2):
        src1[half * 16 : half * 16 + 16] = gram[:, half * RK : half * RK + RK].reshape(16, 8, 128)

    pl.semaphore_wait(barrier, nx * ny - 1 + nz - 1)

    def prepare_right():
        for get in get_right:
            get.wait()
        for p in range(points):
            at = pl.ds(p, 256, stride=points)
            for h in range(2):
                hi, lo = split(rbuf[h, at, :])
                r_hi[p, :, 128 * h : 128 * h + 128] = hi
                r_lo[p, :, 128 * h : 128 * h + 128] = lo

    finish1 = exchange(sizes, src1, sum1, rx1, rz1, sems1, (nothing, nothing, prepare_right))

    work[:, 0:128] = sum1[0:16].reshape(128, 128)
    work[:, 128:256] = sum1[16:32].reshape(128, 128)
    eliminate(work, 2)
    upper = jnp.concatenate([jnp.where(upper_mask(), work[:, 0:128], 0.0), work[:, 128:256]], axis=1)
    up_hi, up_lo = split(upper)
    up_both = jnp.concatenate([up_hi, up_lo], axis=0)
    for p in range(points):
        main = mm(up_both, r_hi[p])
        o = main[:128] + (main[128:] + mm(up_hi, r_lo[p]))
        at = pl.ds(128 * p, 128)
        o_all[at, :] = o
        o_hi[at, :], o_lo[at, :] = split(o)
    cross = mm_tn(o_hi[...], o_lo[...])
    gram = (mm_tn(o_hi[...], o_hi[...]) + (cross + cross.T + mm_tn(o_lo[...], o_lo[...]))) * norm
    for half in range(2):
        src2[16 * half : 16 * half + 16, 0:8] = gram[0:128, 128 * half : 128 * half + 128].reshape(16, 8, 128)
    for k in range(32):
        src2[k, 8:12] = gram[128 + 4 * k : 132 + 4 * k, 128:256]

    def invert():
        work[:, 0:128] = sum1[0:16].reshape(128, 128)
        work[:, 128:256] = identity()
        eliminate(work, 2)

    def place_right():
        for p in range(points):
            for h in range(2):
                rout[h, pl.ds(p, 128, stride=points), :] = o_all[128 * p : 128 * p + 128, 128 * h : 128 * h + 128]

    def make_left():
        w_hi, w_lo = split(work[:, 128:256].T * root)
        weights = jnp.concatenate(
            [jnp.concatenate([w_hi, w_lo], axis=1), jnp.concatenate([w_hi, jnp.zeros_like(w_lo)], axis=1)], axis=0
        )
        for at in spans:
            x_hi, x_lo = split(lbuf[at, 0:128])
            y = mm(jnp.concatenate([x_hi, x_lo], axis=1), weights)
            lout[at, :] = y[:, :128] + y[:, 128:]

    finish2 = exchange(sizes, src2, g2_ref, rx2, rz2, sems2, (invert, place_right, make_left))
    finish1()
    finish2()


def whole(left, right, sizes, points, root, norm):
    rows = left.shape[0]
    out_rows = RK * points
    n, nz = sizes[0] * sizes[1], sizes[2]
    any_spec = pl.BlockSpec(memory_space=pl.ANY)
    return pl.pallas_call(
        functools.partial(whole_kernel, sizes, points, root, norm),
        out_shape=(
            pltpu.VMEM((rows, RK), F32),
            pltpu.VMEM((2, out_rows, 128), F32),
            pltpu.VMEM((n, 12, 128), F32),
        ),
        in_specs=[any_spec, any_spec],
        out_specs=(pl.BlockSpec(memory_space=pltpu.VMEM),) * 3,
        scratch_shapes=[
            pltpu.VMEM((rows, 256), F32),
            pltpu.VMEM((2, right.shape[0], 128), F32),
            pltpu.VMEM((points, 256, 256), BF16),
            pltpu.VMEM((points, 256, 256), BF16),
            pltpu.VMEM((out_rows, 256), BF16),
            pltpu.VMEM((out_rows, 256), BF16),
            pltpu.VMEM((out_rows, 256), F32),
            pltpu.VMEM((128, 256), F32),
            *[pltpu.VMEM((lead, 8, 128), F32) for lead in (n, n, n - 1, nz)],
            *[pltpu.VMEM((lead, 12, 128), F32) for lead in (n, n - 1, nz)],
            pltpu.SemaphoreType.DMA((6,)),
            pltpu.SemaphoreType.DMA((6,)),
            pltpu.SemaphoreType.DMA((6,)),
        ],
        compiler_params=pltpu.CompilerParams(
            collective_id=0, has_side_effects=True, vmem_limit_bytes=56 << 20
        ),
        name="whole",
    )(left, right)


def factor_kernel(g_ref, lo_in, ro_in, f_ref, lo_out, ro_out, work, corner, sem):
    puts = [pltpu.make_async_copy(lo_in, lo_out, sem.at[2])]
    for h in range(2):
        puts.append(pltpu.make_async_copy(ro_in.at[h], ro_out.at[:, 128 * h : 128 * h + 128], sem.at[h]))
    for put in puts:
        put.start()
    work[:, 0:128] = g_ref[0:16, 0:8].reshape(128, 128)
    work[:, 128:256] = g_ref[16:32, 0:8].reshape(128, 128)
    for k in range(32):
        corner[4 * k : 4 * k + 4, :] = g_ref[k, 8:12]
    eliminate(work, 2)
    right = work[:, 128:256]
    f_ref[0:128, 0:128] = jnp.where(upper_mask(), work[:, 0:128], 0.0)
    f_ref[0:128, 128:256] = right
    update = lax.dot_general(
        right, right, (((0,), (0,)), ((), ())), precision=lax.Precision.HIGHEST, preferred_element_type=F32
    )
    work[:, 0:128] = corner[...] - update
    eliminate(work, 1)
    f_ref[128:256, 0:128] = jnp.zeros((128, 128), F32)
    f_ref[128:256, 128:256] = jnp.where(upper_mask(), work[:, 0:128], 0.0)
    for put in puts:
        put.wait()


def factor_and_place(gram, left_out, right_out):
    hbm_spec = pl.BlockSpec(memory_space=pltpu.HBM)
    vmem_spec = pl.BlockSpec(memory_space=pltpu.VMEM)
    return pl.pallas_call(
        factor_kernel,
        out_shape=(
            jax.ShapeDtypeStruct((256, 256), F32),
            jax.ShapeDtypeStruct(left_out.shape, F32),
            jax.ShapeDtypeStruct((right_out.shape[1], 256), F32),
        ),
        in_specs=[vmem_spec] * 3,
        out_specs=(vmem_spec, hbm_spec, hbm_spec),
        scratch_shapes=[pltpu.VMEM((128, 256), F32), pltpu.VMEM((128, 128), F32), pltpu.SemaphoreType.DMA((3,))],
        compiler_params=pltpu.CompilerParams(vmem_limit_bytes=8 << 20),
        name="factor_and_place",
    )(gram, left_out, right_out)


def per_device(left_core, right_core, sizes):
    rank_left, points, rank_mid = left_core.shape
    rank_right = right_core.shape[2]
    total_points = points * sizes[0] * sizes[1] * sizes[2]
    left = left_core.reshape(rank_left * points, rank_mid)
    right = right_core.reshape(rank_mid * points, rank_right)
    root = float(rank_left * total_points) ** 0.5
    norm = 1.0 / (RK * total_points)
    left_out, right_out, gram = whole(left, right, sizes, points, root, norm)
    factor, left_out, right_out = factor_and_place(gram, left_out, right_out)
    return (
        left_out.reshape(rank_left, points, RK),
        right_out.reshape(RK, points, rank_right),
        factor,
    )


def solution(mesh):
    sizes = tuple(mesh.shape[a] for a in ("gx", "gy", "gz"))
    spec = P(None, ("gx", "gy", "gz"), None)
    return jax.shard_map(
        functools.partial(per_device, sizes=sizes),
        mesh=mesh, in_specs=(spec, spec), out_specs=(spec, spec, P()), check_vma=False,
    )
```

```python
import functools

import jax
import jax.numpy as jnp
from jax import lax
from jax.experimental import pallas as pl
from jax.experimental.pallas import tpu as pltpu
from jax.sharding import PartitionSpec as P

RK = 128
F32 = jnp.float32
BF16 = jnp.bfloat16
MESH = pl.DeviceIdType.MESH
AXES = ("gx", "gy", "gz")


def split(x):
    hi = x.astype(BF16)
    return hi, (x - hi.astype(F32)).astype(BF16)


def mm(a, b):
    return lax.dot_general(a, b, (((1,), (0,)), ((), ())), preferred_element_type=F32)


def mm_tn(a, b):
    return lax.dot_general(a, b, (((0,), (0,)), ((), ())), preferred_element_type=F32)


def nothing():
    pass


def near(d, n):
    return min(d, n - d)


def plane(sizes):
    nx, ny, _ = sizes
    chips = nx // 2
    offsets = [(dx, dc, dy) for dx in range(chips) for dc in range(2) for dy in range(ny)][1:]
    offsets.sort(key=lambda o: -near(o[0], chips) - near(o[2], ny))
    gx, gy, gz = (lax.axis_index(a) for a in AXES)
    x, core = lax.div(gx, 2), lax.rem(gx, 2)
    xs = {(dx, dc): lax.rem(x + dx, chips) * 2 + lax.rem(core + dc, 2) for dx in range(chips) for dc in range(2)}
    ys = [lax.rem(gy + dy, ny) for dy in range(ny)]
    return [(xs[dx, dc] * ny + ys[dy], (xs[dx, dc], ys[dy], gz)) for dx, dc, dy in offsets]


def line(sizes):
    nz = sizes[2]
    gx, gy, gz = (lax.axis_index(a) for a in AXES)
    return [(gx, gy, lax.rem(gz + d, nz)) for d in sorted(range(1, nz), key=lambda d: -near(d, nz))]


def exchange(sizes, src, out, rx, rz, sems, hooks):
    nx, ny, nz = sizes
    n = nx * ny
    gz = lax.axis_index("gz")
    me = lax.axis_index("gx") * ny + lax.axis_index("gy")
    in_plane, in_line = plane(sizes), line(sizes)

    def copy(a, b, phase, dev):
        return pltpu.make_async_remote_copy(
            a, b, sems.at[2 * phase], sems.at[2 * phase + 1], device_id=dev, device_id_type=MESH
        )

    for s, (k, dev) in enumerate(in_plane):
        copy(src.at[k], rx.at[s], 0, dev).start()
    hooks[0]()
    scatter = copy(rx, rx, 0, in_plane[0][1])
    scatter.wait_recv()
    total = src[me]
    for s in range(n - 1):
        total = total + rx[s]
    rz[gz] = total
    for dev in in_line:
        copy(rz.at[gz], rz.at[gz], 1, dev).start()
    rest = rz.at[pl.ds(0, nz - 1)]
    across = copy(rest, rest, 1, in_line[0])
    hooks[1]()
    across.wait_recv()
    total = rz[0]
    for z in range(1, nz):
        total = total + rz[z]
    out[me] = total
    for _, dev in in_plane:
        copy(out.at[me], out.at[me], 2, dev).start()
    rest = out.at[pl.ds(0, n - 1)]
    gather = copy(rest, rest, 2, in_plane[0][1])
    hooks[2]()
    gather.wait_recv()

    def finish():
        for waited in (scatter, across, gather):
            waited.wait_send()

    return finish


def eliminate(work, tiles):
    shape = (8, 128)
    sub = lax.broadcasted_iota(jnp.int32, shape, 0)

    def lane(x, c):
        return jnp.take_along_axis(x, jnp.full(shape, c, jnp.int32), axis=1)

    def row(x, i):
        return jnp.take_along_axis(x, jnp.full(shape, i, jnp.int32), axis=0)

    for b in range(16):
        r0 = 8 * b
        rows8 = pl.ds(r0, 8)
        panel = [work[rows8, 128 * t : 128 * t + 128] for t in range(tiles)]

        def lanes(x):
            return [lane(x, r0 + k) for k in range(8)]

        cols = lanes(panel[0])
        e = [[row(cols[k], i) if k <= i else None for k in range(8)] for i in range(8)]
        scale, mult = [], []
        for i in range(8):
            rs = lax.rsqrt(e[i][i])
            l = [None] * 8
            for k in range(i + 1, 8):
                l[k] = e[k][i] * rs
            for k in range(i + 1, 8):
                for j in range(k, 8):
                    e[j][k] = e[j][k] - l[j] * l[k]
            scale.append(rs)
            mult.append(l)

        def forward(v):
            v = list(v)
            for i in range(8):
                v[i] = v[i] * scale[i]
                for k in range(i + 1, 8):
                    v[k] = v[k] - mult[i][k] * v[i]
            return v

        def backward(v):
            v = list(v)
            for i in range(7, -1, -1):
                v[i] = v[i] * scale[i]
                for k in range(i):
                    v[k] = v[k] - mult[k][i] * v[i]
            return v

        rows = [forward([row(p, i) for i in range(8)]) for p in panel]
        for t in range(tiles):
            out = rows[t][0]
            for i in range(1, 8):
                out = jnp.where(sub == i, rows[t][i], out)
            work[rows8, 128 * t : 128 * t + 128] = out
        solved = [backward(r) for r in rows] if tiles > 1 else None
        for m in range(b + 1, 16):
            m8 = pl.ds(8 * m, 8)
            left = lanes(work[m8, 0:128])
            right = rows
            if m == b + 1 or solved is None:
                left = forward(left)
            else:
                right = solved
            for t in range(tiles):
                v = work[m8, 128 * t : 128 * t + 128]
                for k in range(8):
                    v = v - left[k] * right[t][k]
                work[m8, 128 * t : 128 * t + 128] = v


def upper_mask():
    return lax.broadcasted_iota(jnp.int32, (128, 128), 0) <= lax.broadcasted_iota(jnp.int32, (128, 128), 1)


def identity():
    return jnp.where(
        lax.broadcasted_iota(jnp.int32, (128, 128), 0) == lax.broadcasted_iota(jnp.int32, (128, 128), 1), 1.0, 0.0
    ).astype(F32)


def whole_kernel(sizes, points, root, norm, left_hbm, right_hbm, lout, rout, g2_ref,
                 lbuf, rbuf, r_hi, r_lo, o_hi, o_lo, o_all, work, src1, sum1, rx1, rz1, src2, rx2, rz2,
                 sems1, sems2, sem):
    nx, ny, nz = sizes
    rows = lbuf.shape[0]
    bounds = [0, rows // 8, rows * 5 // 16, rows * 19 // 32, rows]
    spans = [pl.ds(lo, hi - lo) for lo, hi in zip(bounds, bounds[1:])]
    get_left = [pltpu.make_async_copy(left_hbm.at[at, :], lbuf.at[at, :], sem.at[c]) for c, at in enumerate(spans)]
    get_right = [
        pltpu.make_async_copy(right_hbm.at[:, 128 * h : 128 * h + 128], rbuf.at[h], sem.at[4 + h]) for h in range(2)
    ]
    for get in get_left:
        get.start()

    barrier = pltpu.get_barrier_semaphore()

    for dev in [dev for _, dev in plane(sizes)] + line(sizes):
        pl.semaphore_signal(barrier, inc=1, device_id=dev, device_id_type=MESH)

    gram = jnp.zeros((RK, 256), F32)
    for get, at in zip(get_left, spans):
        get.wait()
        hi, lo = split(lbuf[at, :])
        both = jnp.concatenate([hi[:, :RK], lo[:, :RK]], axis=1)
        main, cross = mm_tn(both, hi), mm_tn(both, lo)
        gram = gram + (main[:RK] + (main[RK:] + cross[:RK] + cross[RK:]))
    for get in get_right:
        get.start()
    for half in range(2):
        src1[half * 16 : half * 16 + 16] = gram[:, half * RK : half * RK + RK].reshape(16, 8, 128)

    pl.semaphore_wait(barrier, nx * ny - 1 + nz - 1)

    def prepare_right():
        for get in get_right:
            get.wait()
        for p in range(points):
            at = pl.ds(p, 256, stride=points)
            for h in range(2):
                hi, lo = split(rbuf[h, at, :])
                r_hi[p, :, 128 * h : 128 * h + 128] = hi
                r_lo[p, :, 128 * h : 128 * h + 128] = lo

    finish1 = exchange(sizes, src1, sum1, rx1, rz1, sems1, (nothing, nothing, prepare_right))

    work[:, 0:128] = sum1[0:16].reshape(128, 128)
    work[:, 128:256] = sum1[16:32].reshape(128, 128)
    eliminate(work, 2)
    upper = jnp.concatenate([jnp.where(upper_mask(), work[:, 0:128], 0.0), work[:, 128:256]], axis=1)
    up_hi, up_lo = split(upper)
    up_both = jnp.concatenate([up_hi, up_lo], axis=0)
    for p in range(points):
        main = mm(up_both, r_hi[p])
        o = main[:128] + (main[128:] + mm(up_hi, r_lo[p]))
        at = pl.ds(128 * p, 128)
        o_all[at, :] = o
        o_hi[at, :], o_lo[at, :] = split(o)
    cross = mm_tn(o_hi[...], o_lo[...])
    gram = (mm_tn(o_hi[...], o_hi[...]) + (cross + cross.T + mm_tn(o_lo[...], o_lo[...]))) * norm
    for half in range(2):
        src2[16 * half : 16 * half + 16, 0:8] = gram[0:128, 128 * half : 128 * half + 128].reshape(16, 8, 128)
    for k in range(32):
        src2[k, 8:12] = gram[128 + 4 * k : 132 + 4 * k, 128:256]

    def invert():
        work[:, 0:128] = sum1[0:16].reshape(128, 128)
        work[:, 128:256] = identity()
        eliminate(work, 2)

    def place_right():
        for p in range(points):
            for h in range(2):
                rout[h, pl.ds(p, 128, stride=points), :] = o_all[128 * p : 128 * p + 128, 128 * h : 128 * h + 128]

    def make_left():
        w_hi, w_lo = split(work[:, 128:256].T * root)
        weights = jnp.concatenate(
            [jnp.concatenate([w_hi, w_lo], axis=1), jnp.concatenate([w_hi, jnp.zeros_like(w_lo)], axis=1)], axis=0
        )
        for at in spans:
            x_hi, x_lo = split(lbuf[at, 0:128])
            y = mm(jnp.concatenate([x_hi, x_lo], axis=1), weights)
            lout[at, :] = y[:, :128] + y[:, 128:]

    finish2 = exchange(sizes, src2, g2_ref, rx2, rz2, sems2, (invert, place_right, make_left))
    finish1()
    finish2()


def whole(left, right, sizes, points, root, norm):
    rows = left.shape[0]
    out_rows = RK * points
    n, nz = sizes[0] * sizes[1], sizes[2]
    any_spec = pl.BlockSpec(memory_space=pl.ANY)
    return pl.pallas_call(
        functools.partial(whole_kernel, sizes, points, root, norm),
        out_shape=(
            pltpu.VMEM((rows, RK), F32),
            pltpu.VMEM((2, out_rows, 128), F32),
            pltpu.VMEM((n, 12, 128), F32),
        ),
        in_specs=[any_spec, any_spec],
        out_specs=(pl.BlockSpec(memory_space=pltpu.VMEM),) * 3,
        scratch_shapes=[
            pltpu.VMEM((rows, 256), F32),
            pltpu.VMEM((2, right.shape[0], 128), F32),
            pltpu.VMEM((points, 256, 256), BF16),
            pltpu.VMEM((points, 256, 256), BF16),
            pltpu.VMEM((out_rows, 256), BF16),
            pltpu.VMEM((out_rows, 256), BF16),
            pltpu.VMEM((out_rows, 256), F32),
            pltpu.VMEM((128, 256), F32),
            *[pltpu.VMEM((lead, 8, 128), F32) for lead in (n, n, n - 1, nz)],
            *[pltpu.VMEM((lead, 12, 128), F32) for lead in (n, n - 1, nz)],
            pltpu.SemaphoreType.DMA((6,)),
            pltpu.SemaphoreType.DMA((6,)),
            pltpu.SemaphoreType.DMA((6,)),
        ],
        compiler_params=pltpu.CompilerParams(
            collective_id=0, has_side_effects=True, vmem_limit_bytes=56 << 20
        ),
        name="whole",
    )(left, right)


def factor_kernel(g_ref, lo_in, ro_in, f_out, lo_out, ro_out, f_ref, work, corner, sem):
    puts = [pltpu.make_async_copy(lo_in, lo_out, sem.at[2])]
    for h in range(2):
        puts.append(pltpu.make_async_copy(ro_in.at[h], ro_out.at[:, 128 * h : 128 * h + 128], sem.at[h]))
    for put in puts:
        put.start()
    work[:, 0:128] = g_ref[0:16, 0:8].reshape(128, 128)
    work[:, 128:256] = g_ref[16:32, 0:8].reshape(128, 128)
    for k in range(32):
        corner[4 * k : 4 * k + 4, :] = g_ref[k, 8:12]
    eliminate(work, 2)
    right = work[:, 128:256]
    f_ref[0:128, 0:128] = jnp.where(upper_mask(), work[:, 0:128], 0.0)
    f_ref[0:128, 128:256] = right
    f_ref[128:256, 0:128] = jnp.zeros((128, 128), F32)
    parts = [(pl.ds(0, 128), pl.ds(0, 256)), (pl.ds(128, 128), pl.ds(0, 128)), (pl.ds(128, 128), pl.ds(128, 128))]
    for i, at in enumerate(parts):
        puts.append(pltpu.make_async_copy(f_ref.at[at], f_out.at[at], sem.at[3 + i]))
    for put in puts[-3:-1]:
        put.start()
    update = lax.dot_general(
        right, right, (((0,), (0,)), ((), ())), precision=lax.Precision.HIGHEST, preferred_element_type=F32
    )
    work[:, 0:128] = corner[...] - update
    eliminate(work, 1)
    f_ref[128:256, 128:256] = jnp.where(upper_mask(), work[:, 0:128], 0.0)
    puts[-1].start()
    for put in puts:
        put.wait()


def factor_and_place(gram, left_out, right_out):
    hbm_spec = pl.BlockSpec(memory_space=pltpu.HBM)
    vmem_spec = pl.BlockSpec(memory_space=pltpu.VMEM)
    return pl.pallas_call(
        factor_kernel,
        out_shape=(
            jax.ShapeDtypeStruct((256, 256), F32),
            jax.ShapeDtypeStruct(left_out.shape, F32),
            jax.ShapeDtypeStruct((right_out.shape[1], 256), F32),
        ),
        in_specs=[vmem_spec] * 3,
        out_specs=(hbm_spec, hbm_spec, hbm_spec),
        scratch_shapes=[
            pltpu.VMEM((256, 256), F32),
            pltpu.VMEM((128, 256), F32),
            pltpu.VMEM((128, 128), F32),
            pltpu.SemaphoreType.DMA((6,)),
        ],
        compiler_params=pltpu.CompilerParams(vmem_limit_bytes=8 << 20),
        name="factor_and_place",
    )(gram, left_out, right_out)


def per_device(left_core, right_core, sizes):
    rank_left, points, rank_mid = left_core.shape
    rank_right = right_core.shape[2]
    total_points = points * sizes[0] * sizes[1] * sizes[2]
    left = left_core.reshape(rank_left * points, rank_mid)
    right = right_core.reshape(rank_mid * points, rank_right)
    root = float(rank_left * total_points) ** 0.5
    norm = 1.0 / (RK * total_points)
    left_out, right_out, gram = whole(left, right, sizes, points, root, norm)
    factor, left_out, right_out = factor_and_place(gram, left_out, right_out)
    return (
        left_out.reshape(rank_left, points, RK),
        right_out.reshape(RK, points, rank_right),
        factor,
    )


def solution(mesh):
    sizes = tuple(mesh.shape[a] for a in ("gx", "gy", "gz"))
    spec = P(None, ("gx", "gy", "gz"), None)
    return jax.shard_map(
        functools.partial(per_device, sizes=sizes),
        mesh=mesh, in_specs=(spec, spec), out_specs=(spec, spec, P()), check_vma=False,
    )
```
